32 devices in a mesh: fsdp: 4 (over y, x), ctx: 8 (over z, core).
Axes of the slice: x: 2, y: 2, z: 4, core: 2. Of those that a mesh axis runs over, the one named last changes fastest.
Arguments:
- layer_input: bfloat16 [4, 2048, 2048], P('fsdp', 'ctx'), may hold values from -6 to 6
- lengths: int32 [4], P('fsdp'), may hold values from 1024 to 2048, as said below
- order: int32 [4], P('fsdp'), may hold values from 0 to 3, as said below
- offsets: int32 [4, 16], P('fsdp', 'ctx'), may hold values from 0 to 1920, as said below
- attn_gain: bfloat16 [2048], P(('fsdp', 'ctx')), may hold values from 0.25 to 1.75
- w_query: bfloat16 [2048, 2048], P(('fsdp', 'ctx')), may hold values from -0.125 to 0.125
- w_key: bfloat16 [2048, 1024], P(('fsdp', 'ctx')), may hold values from -0.125 to 0.125
- w_value: bfloat16 [2048, 1024], P(('fsdp', 'ctx')), may hold values from -0.125 to 0.125
- q_gain: bfloat16 [128], P(('fsdp', 'ctx')), may hold values from 1 to 1.796875
- k_gain: bfloat16 [128], P(('fsdp', 'ctx')), may hold values from 1 to 1.796875
- w_out: bfloat16 [2048, 2048], P(('fsdp', 'ctx')), may hold values from -0.75 to 0.75
- mlp_gain: bfloat16 [2048], P(('fsdp', 'ctx')), may hold values from 0.25 to 1.75
- w_gate: bfloat16 [2048, 6144], P(('fsdp', 'ctx')), may hold values from -0.125 to 0.125
- w_up: bfloat16 [2048, 6144], P(('fsdp', 'ctx')), may hold values from -0.125 to 0.125
- w_down: bfloat16 [6144, 2048], P(('fsdp', 'ctx')), may hold values from -0.078125 to 0.078125
- grad_out: bfloat16 [4, 2048, 2048], P('fsdp', 'ctx'), may hold values from -6 to 6
Outputs:
- layer_output: bfloat16 [4, 2048, 2048], P('fsdp', 'ctx')
- grad_x: bfloat16 [4, 2048, 2048], P('fsdp', 'ctx')
- grad_attn_gain: float32 [2048], P(('fsdp', 'ctx'))
- grad_w_query: float32 [2048, 2048], P(('fsdp', 'ctx'))
- grad_w_key: float32 [2048, 1024], P(('fsdp', 'ctx'))
- grad_w_value: float32 [2048, 1024], P(('fsdp', 'ctx'))
- grad_q_gain: float32 [128], P(('fsdp', 'ctx'))
- grad_k_gain: float32 [128], P(('fsdp', 'ctx'))
- grad_w_out: float32 [2048, 2048], P(('fsdp', 'ctx'))
- grad_mlp_gain: float32 [2048], P(('fsdp', 'ctx'))
- grad_w_gate: float32 [2048, 6144], P(('fsdp', 'ctx'))
- grad_w_up: float32 [2048, 6144], P(('fsdp', 'ctx'))
- grad_w_down: float32 [6144, 2048], P(('fsdp', 'ctx'))
The draws below stay inside these ranges and needn't reach their ends.
Inputs may be any that keep to these rules, and one draw needn't show every extreme that they name: `lengths`: rows at or past a sequence's length are padding; some sequence has exactly 2048 positions and some exactly 1024. `order`: a permutation; entries g * 1 to (g + 1) - 1 name the sequences placed in the group of fsdp index g. For every sequence, ctx index d stores blocks 2d and 2d+1 of 128 rows, with offsets p * 128 and (15 - p) * 128 for a p that differs between the devices of ctx, so each position is stored once.
All inputs are finite; a program needn't handle non-finite values.
Results may differ from the reference program's by a relative error of at most 0.02.
Values may be sent and summed in bfloat16 or wider, within the bound.
A program may use at most 384 MiB of HBM per device.

```python
import math
import jax
import jax.numpy as jnp
from jax import lax

D = 2048
H = 16
KVH = 8
HD = 128
FF = 6144
SLOT = 2048
SEQ_GRP = 1
NSEQ = 4
BLOCKS = 16
BLOCK = 128
N_CTX = 8


def lengths_and_order(key):
    count = NSEQ
    seq_index = jnp.arange(count, dtype=jnp.int32)
    drawn = jax.random.randint(jax.random.fold_in(key, 11), (count,), SLOT // 2, SLOT + 1, dtype=jnp.int32)
    longest = jax.random.randint(jax.random.fold_in(key, 12), (), 0, count, dtype=jnp.int32)
    shortest = (longest + 1 + jax.random.randint(jax.random.fold_in(key, 13), (), 0, count - 1, dtype=jnp.int32)) % count
    drawn = jnp.where(seq_index == longest, SLOT, jnp.where(seq_index == shortest, SLOT // 2, drawn))
    ranks = jax.random.permutation(jax.random.fold_in(key, 14), count).astype(jnp.int32)
    ranked = jnp.argsort(-(drawn * count + ranks)).astype(jnp.int32)
    group_count = count // SEQ_GRP
    round_number = seq_index // group_count
    within = seq_index % group_count
    group_id = jnp.where(round_number % 2 == 0, within, group_count - 1 - within)
    target = group_id * SEQ_GRP + round_number
    placed = jnp.zeros((count,), jnp.int32).at[target].set(ranked)
    return (drawn, placed)


def draw_lengths(key, part):
    return lengths_and_order(key)[0]


def draw_order(key, part):
    return lengths_and_order(key)[1]


def draw_offsets(key, part):
    pair_count = BLOCKS // 2
    seq_keys = jax.random.split(jax.random.fold_in(key, 21), NSEQ)
    dealt = jax.vmap(lambda single: jax.random.permutation(single, pair_count))(seq_keys).astype(jnp.int32)
    lower = dealt * BLOCK
    upper = (BLOCKS - 1 - dealt) * BLOCK
    return jnp.stack([lower, upper], axis=-1).reshape(NSEQ, BLOCKS)


def steps_of(stream_key, shape, cuts, least, high):
    def one(axis_at, blocks):
        heights = jax.random.uniform(jax.random.fold_in(jax.random.fold_in(stream_key, 6), axis_at), (blocks,), jnp.float32, least / len(cuts), high / len(cuts))
        return jnp.repeat(jnp.exp(heights), shape[axis_at] // blocks).reshape((-1,) + (1,) * (len(shape) - axis_at - 1))

    loudness = one(*cuts[0])
    for cut in cuts[1:]:
        loudness = loudness * one(*cut)
    return loudness


def scatter_about(key, shape, deviation, most, pieces=(), kind=jnp.bfloat16):
    factor_of = steps_of(key, shape, pieces, -0.22, 0.18) if pieces else 1.0
    entries = jax.random.normal(key, shape, jnp.float32) * deviation * factor_of
    return jnp.minimum(jnp.maximum(entries, -most), most).astype(kind)


def setup_inputs(seed: int = 0) -> dict:
    seeds = jax.random.split(jax.random.key(seed), 17)
    return {
        "layer_input": scatter_about(seeds[0], (NSEQ, SLOT, D), 1.0, 6.0, ((0, 4), (1, 8))),
        "lengths": draw_lengths(jax.random.fold_in(seeds[16], 71), 0),
        "order": draw_order(jax.random.fold_in(seeds[16], 71), 0),
        "offsets": draw_offsets(jax.random.fold_in(seeds[16], 71), 0),
        "attn_gain": jnp.clip(1.0 + 0.15 * jax.random.normal(seeds[4], (D,), jnp.float32), 0.25, 1.75).astype(jnp.bfloat16),
        "w_query": scatter_about(seeds[5], (D, H * HD), D ** -0.5, 0.125, ((0, 32),)),
        "w_key": scatter_about(seeds[6], (D, KVH * HD), D ** -0.5, 0.125, ((0, 32),)),
        "w_value": scatter_about(seeds[7], (D, KVH * HD), D ** -0.5, 0.125, ((0, 32),)),
        "q_gain": jnp.clip(jnp.exp(math.log(1.796875) - 0.586049 * jax.random.uniform(seeds[8], (HD,), jnp.float32) ** steps_of(seeds[8], (HD,), ((0, 32),), -0.2, 0.2)), 1.0, 1.796875).astype(jnp.bfloat16),
        "k_gain": jnp.clip(jnp.exp(math.log(1.796875) - 0.586049 * jax.random.uniform(seeds[9], (HD,), jnp.float32) ** steps_of(seeds[9], (HD,), ((0, 32),), -0.2, 0.2)), 1.0, 1.796875).astype(jnp.bfloat16),
        "w_out": scatter_about(seeds[10], (H * HD, D), (H * HD // 32) ** -0.5, 0.75, ((0, 32),)),
        "mlp_gain": jnp.clip(1.0 + 0.15 * jax.random.normal(seeds[11], (D,), jnp.float32), 0.25, 1.75).astype(jnp.bfloat16),
        "w_gate": scatter_about(seeds[12], (D, FF), D ** -0.5, 0.125, ((0, 32),)),
        "w_up": scatter_about(seeds[13], (D, FF), D ** -0.5, 0.125, ((0, 32),)),
        "w_down": scatter_about(seeds[14], (FF, D), FF ** -0.5, 0.078125, ((0, 32),)),
        "grad_out": scatter_about(seeds[15], (NSEQ, SLOT, D), 1.0, 6.0, ((0, 4), (1, 8))),
    }


EPS = 1e-06
THETA = 1000000.0
NEG = -1e+30

@jax.custom_vjp
def low(v):
    return lax.optimization_barrier(v.astype(jnp.bfloat16)).astype(jnp.float32)

@jax.custom_vjp
def low_back(v):
    return v

def low_keep(v):
    return (low(v), None)

def low_pass(kept, grad):
    return (grad,)

def back_keep(v):
    return (v, None)

def back_low(kept, grad):
    return (low(grad),)
low.defvjp(low_keep, low_pass)
low_back.defvjp(back_keep, back_low)

def rms_scale(values, gain):
    inverse = lax.rsqrt(lax.optimization_barrier(jnp.mean(values * values, axis=-1, keepdims=True)) + EPS)
    return values * inverse * gain

def rope_tables(positions, width):
    half_width = width // 2
    freqs = THETA ** (-(jnp.arange(half_width, dtype=jnp.float32) * 2.0) / width)
    angles = positions.astype(jnp.float32)[..., None] * freqs
    cosine = jnp.cos(angles)
    sine = jnp.sin(angles)
    return (jnp.concatenate([cosine, cosine], axis=-1), jnp.concatenate([sine, sine], axis=-1))

def rotate(vectors, cosine, sine):
    half_width = vectors.shape[-1] // 2
    turned = jnp.concatenate([-vectors[..., half_width:], vectors[..., :half_width]], axis=-1)
    return vectors * cosine + turned * sine

def head_path(projection, gain, cosine, sine):
    seq_count, row_count, width_all = projection.shape
    split = projection.reshape(seq_count, row_count, width_all // gain.shape[0], gain.shape[0])
    return rotate(rms_scale(split, gain), cosine[:, :, None, :], sine[:, :, None, :])

def project(left, right):
    return jnp.dot(left, right, precision=lax.Precision.HIGHEST, preferred_element_type=jnp.float32)

def one_sequence(items):
    query_one, key_one, value_one, positions_one, length_one = items
    row_count = query_one.shape[0]
    queries = query_one.reshape(row_count, KVH, H // KVH, HD)
    raw_scores = jnp.einsum('rkgd,tkd->kgrt', queries, key_one, precision=lax.Precision.HIGHEST)
    scores = low_back(raw_scores * HD ** (-0.5))
    allowed = (positions_one[None, :] <= positions_one[:, None]) & (positions_one[None, :] < length_one)
    scores = jnp.where(allowed[None, None], scores, NEG)
    row_top = lax.optimization_barrier(jnp.max(scores, axis=-1, keepdims=True))
    exponent = jnp.exp(scores - row_top)
    probs = exponent / lax.optimization_barrier(jnp.sum(exponent, axis=-1, keepdims=True))
    mixture = jnp.einsum('kgrt,tkd->rkgd', low(probs), value_one, precision=lax.Precision.HIGHEST)
    return mixture.reshape(row_count, H * HD)

def forward(resid, positions, seq_lengths, attn_gain, w_query, w_key, w_value, q_gain, k_gain, w_out, mlp_gain, w_gate, w_up, w_down):
    seq_count, slot_rows, width_all = resid.shape
    flat = resid.reshape(seq_count * slot_rows, width_all)
    cosine, sine = rope_tables(positions, HD)
    normed_one = low(rms_scale(flat, attn_gain))
    query_proj = low_back(project(normed_one, w_query))
    key_proj = low_back(project(normed_one, w_key))
    value_proj = low(low_back(project(normed_one, w_value)))
    query_rot = low(head_path(query_proj.reshape(seq_count, slot_rows, -1), q_gain, cosine, sine))
    key_rot = low(head_path(key_proj.reshape(seq_count, slot_rows, -1), k_gain, cosine, sine))
    value_heads = value_proj.reshape(seq_count, slot_rows, KVH, HD)
    mixture = lax.map(jax.checkpoint(one_sequence), (query_rot, key_rot, value_heads, positions, seq_lengths))
    mix_round = low(low_back(mixture.reshape(seq_count * slot_rows, H * HD)))
    hidden_res = flat + low_back(project(mix_round, w_out))
    normed_two = low(rms_scale(hidden_res, mlp_gain))
    gate_proj = low_back(project(normed_two, w_gate))
    up_proj = low_back(project(normed_two, w_up))
    hidden_act = low(jax.nn.silu(gate_proj) * up_proj)
    output = hidden_res + low_back(project(hidden_act, w_down))
    return output.reshape(seq_count, slot_rows, width_all)

def reference(layer_input, lengths, order, offsets, attn_gain, w_query, w_key, w_value, q_gain, k_gain, w_out, mlp_gain, w_gate, w_up, w_down, grad_out):
    block_rows = SLOT // (2 * N_CTX)
    seq_lengths = jnp.take(lengths, order)
    seq_offsets = jnp.take(offsets, order, axis=0)
    slot_index = jnp.arange(SLOT, dtype=jnp.int32)
    positions = jnp.take(seq_offsets, slot_index // block_rows, axis=1) + slot_index % block_rows
    valid = positions < seq_lengths[:, None]
    floats = [value.astype(jnp.float32) for value in (layer_input, attn_gain, w_query, w_key, w_value, q_gain, k_gain, w_out, mlp_gain, w_gate, w_up, w_down)]

    def run(input_given, *weights):
        return forward(jnp.take(input_given, order, axis=0), positions, seq_lengths, *weights)
    output, pullback = jax.vjp(run, *floats)
    cotangent = grad_out.astype(jnp.float32) * valid[:, :, None].astype(jnp.float32)
    gradients = pullback(cotangent)
    return (output.astype(jnp.bfloat16), gradients[0].astype(jnp.bfloat16), gradients[1], gradients[2], gradients[3], gradients[4], gradients[5], gradients[6], gradients[7], gradients[8], gradients[9], gradients[10], gradients[11])
```

```python
import functools

import jax
import jax.numpy as jnp
from jax import lax
from jax.sharding import PartitionSpec as P

H = 16
KVH = 8
HD = 128

EPS = 1e-06
THETA = 1000000.0
NEG = -1e30
BF = jnp.bfloat16
F32 = jnp.float32


def rms_scale(values, gain):
    inverse = lax.rsqrt(jnp.mean(values * values, axis=-1, keepdims=True) + EPS)
    return values * inverse * gain


def rope_tables(positions, width):
    half_width = width // 2
    freqs = THETA ** (-(jnp.arange(half_width, dtype=F32) * 2.0) / width)
    angles = positions.astype(F32)[..., None] * freqs
    cosine = jnp.cos(angles)
    sine = jnp.sin(angles)
    return (jnp.concatenate([cosine, cosine], axis=-1), jnp.concatenate([sine, sine], axis=-1))


def rotate(vectors, cosine, sine):
    half_width = vectors.shape[-1] // 2
    turned = jnp.concatenate([-vectors[..., half_width:], vectors[..., :half_width]], axis=-1)
    return vectors * cosine + turned * sine


def head_path(projection, gain, cosine, sine):
    seqs, rows, width_all = projection.shape
    split = projection.reshape(seqs, rows, width_all // HD, HD)
    return rotate(rms_scale(split, gain), cosine[:, :, None, :], sine[:, :, None, :])


def dot_nn(left, right):
    return lax.dot_general(left, right, (((1,), (0,)), ((), ())), preferred_element_type=F32)


def dot_nt(left, right):
    return lax.dot_general(left, right, (((1,), (1,)), ((), ())), preferred_element_type=F32)


def dot_tn(left, right):
    return lax.dot_general(left, right, (((0,), (0,)), ((), ())), preferred_element_type=F32)


def swap(block, step, count):
    if step == 0:
        return block
    return lax.ppermute(block, "fsdp", [(i, i ^ step) for i in range(count)])


def pick(stacked, index):
    return lax.dynamic_index_in_dim(stacked, index, 0, keepdims=False)


def per_device(
    layer_input,
    lengths,
    order,
    offsets,
    attn_gain,
    w_query,
    w_key,
    w_value,
    q_gain,
    k_gain,
    w_out,
    mlp_gain,
    w_gate,
    w_up,
    w_down,
    grad_out,
):
    groups, ring = lax.axis_size("fsdp"), lax.axis_size("ctx")
    _, rows, width = layer_input.shape
    block_rows = rows // 2
    heads, kv_heads = H // groups, KVH // groups
    per_key = H // KVH
    q_width, kv_width = heads * HD, kv_heads * HD
    shard_rows = w_query.shape[0]
    hidden = w_gate.shape[1] // groups
    score_scale = HD ** (-0.5)
    own = lax.axis_index("fsdp")
    own_ctx = lax.axis_index("ctx")
    steps = range(groups)
    tokens = groups * rows

    small = jnp.concatenate(
        [
            attn_gain.astype(F32),
            mlp_gain.astype(F32),
            q_gain.astype(F32),
            k_gain.astype(F32),
            lengths.astype(F32),
            order.astype(F32),
            offsets.reshape(-1).astype(F32),
        ]
    )[None, :]
    small_all = lax.all_gather(small, ("fsdp", "ctx"), axis=0, tiled=True)
    gain_rows, head_rows = attn_gain.shape[0], q_gain.shape[0]
    at = 0
    attn_gain_full = small_all[:, at : at + gain_rows].reshape(-1)
    at += gain_rows
    mlp_gain_full = small_all[:, at : at + gain_rows].reshape(-1)
    at += gain_rows
    q_gain_full = small_all[:, at : at + head_rows].reshape(-1)
    at += head_rows
    k_gain_full = small_all[:, at : at + head_rows].reshape(-1)
    at += head_rows
    whole = small_all[:, at:].astype(jnp.int32).reshape(groups, ring, 4)
    lengths_all = whole[:, 0, 0]
    order_all = whole[:, 0, 1]
    offsets_all = whole[:, :, 2:4]
    near = own ^ jnp.arange(groups, dtype=jnp.int32)
    length_of = lengths_all[near]
    row_index = jnp.arange(rows, dtype=jnp.int32)
    key_positions = (
        jnp.where(
            (row_index < block_rows)[None, None, :],
            offsets_all[near][:, :, 0:1],
            offsets_all[near][:, :, 1:2],
        )
        + row_index % block_rows
    )
    positions = lax.dynamic_index_in_dim(key_positions, own_ctx, 1, keepdims=False)
    key_positions = key_positions.reshape(groups, -1)
    valid = positions < length_of[:, None]
    slot_of = jnp.sum(
        jnp.where(order_all[None, :] == near[:, None], jnp.arange(groups, dtype=jnp.int32)[None, :], 0), axis=1
    )
    seq_at = order_all[near]

    def to_columns(parts):
        out = jnp.zeros((groups, shard_rows, sum(p.shape[1] for p in parts) // groups), BF)
        for k in steps:
            piece = jnp.concatenate(
                [
                    lax.dynamic_slice_in_dim(p, (own ^ k) * (p.shape[1] // groups), p.shape[1] // groups, 1)
                    for p in parts
                ],
                axis=1,
            )
            out = lax.dynamic_update_index_in_dim(out, swap(piece, k, groups), own ^ k, 0)
        return out

    def from_columns(grad, widths):
        outs = [jnp.zeros((shard_rows, w * groups), F32) for w in widths]
        for k in steps:
            piece = swap(pick(grad, own ^ k), k, groups).astype(F32)
            at = 0
            for n, w in enumerate(widths):
                outs[n] = lax.dynamic_update_slice_in_dim(outs[n], piece[:, at : at + w], (own ^ k) * w, 1)
                at += w
        return outs

    x_own = layer_input[0]
    qkv_local = to_columns([w_query, w_key, w_value])
    w_qkv = lax.all_gather(qkv_local, "ctx", axis=1, tiled=True).reshape(width, -1)
    x_all = jnp.stack([swap(x_own, k, groups) for k in steps])
    flat = x_all.reshape(tokens, width).astype(F32)
    normed_one = rms_scale(flat, attn_gain_full).astype(BF)
    cosine, sine = rope_tables(positions, HD)
    qkv = dot_nn(normed_one, w_qkv).reshape(groups, rows, -1)
    query_proj = qkv[:, :, :q_width]
    key_proj = qkv[:, :, q_width : q_width + kv_width]
    value_b = qkv[:, :, q_width + kv_width :].astype(BF)
    query_rot = head_path(query_proj, q_gain_full, cosine, sine).astype(BF)
    key_rot = head_path(key_proj, k_gain_full, cosine, sine).astype(BF).reshape(groups, rows, -1)
    kv_all = lax.all_gather(jnp.concatenate([key_rot, value_b], axis=2), "ctx", axis=1, tiled=True)
    w_out_full = lax.all_gather(w_out, "ctx", axis=0, tiled=True)
    gate_up_local = to_columns([w_gate, w_up])
    w_gate_up = lax.all_gather(gate_up_local, "ctx", axis=1, tiled=True).reshape(width, -1)
    w_down_full = lax.all_gather(w_down, "ctx", axis=0, tiled=True)

    queries = query_rot.reshape(groups, rows, kv_heads, per_key, HD)
    keys = kv_all[:, :, :kv_width].reshape(groups, -1, kv_heads, HD)
    values = kv_all[:, :, kv_width:].reshape(groups, -1, kv_heads, HD)
    allowed = (key_positions[:, None, :] <= positions[:, :, None]) & (
        key_positions[:, None, :] < length_of[:, None, None]
    )

    def scores_of():
        raw = jnp.einsum("srkgd,stkd->skgrt", queries, keys, preferred_element_type=F32)
        return jnp.where(allowed[:, None, None], raw * score_scale, NEG)

    scores = scores_of()
    row_top = jnp.max(scores, axis=-1, keepdims=True)
    exponent = jnp.exp(scores - row_top)
    row_total = jnp.sum(exponent, axis=-1, keepdims=True)
    probs = (exponent / row_total).astype(BF)
    mixture = jnp.einsum("skgrt,stkd->srkgd", probs, values, preferred_element_type=F32)
    mix_b = mixture.reshape(tokens, -1).astype(BF)
    log_totals = row_top + jnp.log(row_total)

    attn_part = dot_nn(mix_b, w_out_full).reshape(groups, rows, width)
    hidden_res = x_own.astype(F32) + attn_part[0]
    for k in steps[1:]:
        hidden_res = hidden_res + swap(attn_part[k].astype(BF), k, groups).astype(F32)
    normed_two_own = rms_scale(hidden_res, mlp_gain_full).astype(BF)
    normed_two = jnp.concatenate([swap(normed_two_own, k, groups) for k in steps], axis=0)
    gate_up = dot_nn(normed_two, w_gate_up)
    gate_proj, up_proj = gate_up[:, :hidden], gate_up[:, hidden:]
    hidden_act = (jax.nn.silu(gate_proj) * up_proj).astype(BF)
    out_part = dot_nn(hidden_act, w_down_full).reshape(groups, rows, width)
    out_part = jnp.concatenate([(out_part[:1] + hidden_res[None]).astype(BF), out_part[1:].astype(BF)], axis=0)
    result = pick(out_part, own ^ seq_at[0]).astype(F32)
    for k in steps[1:]:
        result = result + swap(pick(out_part, own ^ seq_at[k]), k, groups).astype(F32)
    result = result.astype(BF)[None]

    dy_slots = jnp.stack([swap(grad_out[0], k, groups) for k in steps])
    dy_b = jnp.concatenate(
        [jnp.where(valid[k][:, None], pick(dy_slots, own ^ slot_of[k]), jnp.zeros((), BF)) for k in steps], axis=0
    )
    dhid = dot_nt(dy_b, w_down_full)
    _, swiglu_pull = jax.vjp(lambda g, u: jax.nn.silu(g) * u, gate_proj, up_proj)
    dgate_f, dup_f = swiglu_pull(dhid)
    dgate_up = jnp.concatenate([dgate_f.astype(BF), dup_f.astype(BF)], axis=1)
    dn_two_part = dot_nt(dgate_up, w_gate_up).reshape(groups, rows, width)
    grad_down = lax.psum_scatter(dot_tn(hidden_act, dy_b).astype(BF), "ctx", scatter_dimension=0, tiled=True)
    dn_two = dn_two_part[0]
    for k in steps[1:]:
        dn_two = dn_two + swap(dn_two_part[k].astype(BF), k, groups).astype(F32)
    _, norm_two_pull = jax.vjp(rms_scale, hidden_res, mlp_gain_full)
    dh_norm, dmlp_gain_part = norm_two_pull(dn_two)
    dh_rows = dy_b[:rows].astype(F32) + dh_norm
    dattn_own = dh_rows.astype(BF)
    dattn_b = jnp.concatenate([swap(dattn_own, k, groups) for k in steps], axis=0)
    grad_gate_up = lax.psum_scatter(
        dot_tn(normed_two, dgate_up).astype(BF).reshape(groups, -1, 2 * hidden),
        "ctx",
        scatter_dimension=1,
        tiled=True,
    )
    dmix_b = dot_nt(dattn_b, w_out_full).astype(BF)
    grad_out_w = lax.psum_scatter(dot_tn(mix_b, dattn_b).astype(BF), "ctx", scatter_dimension=0, tiled=True)

    dmix_heads = dmix_b.reshape(groups, rows, kv_heads, per_key, HD)
    attn_probs = jnp.exp(scores_of() - log_totals)
    probs_b = attn_probs.astype(BF)
    dprob = jnp.einsum("srkgd,stkd->skgrt", dmix_heads, values, preferred_element_type=F32)
    delta = jnp.sum(attn_probs * dprob, axis=-1, keepdims=True)
    dscore = (attn_probs * (dprob - delta)).astype(BF)
    dq_rot = jnp.einsum("skgrt,stkd->srkgd", dscore, keys, preferred_element_type=F32) * score_scale
    dk_part = jnp.einsum("skgrt,srkgd->stkd", dscore, queries, preferred_element_type=F32) * score_scale
    dv_part = jnp.einsum("skgrt,srkgd->stkd", probs_b, dmix_heads, preferred_element_type=F32)
    dkv_part = jnp.concatenate(
        [dk_part.reshape(groups, -1, kv_width).astype(BF), dv_part.reshape(groups, -1, kv_width).astype(BF)], axis=2
    )
    dkv = lax.psum_scatter(dkv_part, "ctx", scatter_dimension=1, tiled=True)
    _, query_pull = jax.vjp(lambda p, g: head_path(p, g, cosine, sine), query_proj, q_gain_full)
    dq_proj, dq_gain_part = query_pull(dq_rot.reshape(groups, rows, heads, HD))
    _, key_pull = jax.vjp(lambda p, g: head_path(p, g, cosine, sine), key_proj, k_gain_full)
    dk_proj, dk_gain_part = key_pull(dkv[:, :, :kv_width].astype(F32).reshape(groups, rows, kv_heads, HD))
    dqkv = jnp.concatenate([dq_proj.astype(BF), dk_proj.astype(BF), dkv[:, :, kv_width:]], axis=2).reshape(tokens, -1)
    dn_one_part = dot_nt(dqkv, w_qkv).reshape(groups, rows, width)
    dn_one = dn_one_part[0]
    for k in steps[1:]:
        dn_one = dn_one + swap(dn_one_part[k].astype(BF), k, groups).astype(F32)
    grad_qkv = lax.psum_scatter(
        dot_tn(normed_one, dqkv).astype(BF).reshape(groups, -1, dqkv.shape[1]),
        "ctx",
        scatter_dimension=1,
        tiled=True,
    )
    _, norm_one_pull = jax.vjp(rms_scale, x_own.astype(F32), attn_gain_full)
    dflat_norm, dattn_gain_part = norm_one_pull(dn_one)
    grad_x = (dh_rows + dflat_norm).astype(BF)[None]

    devices = groups * ring
    gains = jnp.concatenate(
        [
            dattn_gain_part.reshape(devices, -1),
            dmlp_gain_part.reshape(devices, -1),
            dq_gain_part.reshape(devices, -1),
            dk_gain_part.reshape(devices, -1),
        ],
        axis=1,
    )
    gains = lax.psum_scatter(gains, ("fsdp", "ctx"), scatter_dimension=0, tiled=True)[0]
    grad_attn_gain = gains[:gain_rows]
    grad_mlp_gain = gains[gain_rows : 2 * gain_rows]
    grad_q_gain = gains[2 * gain_rows : 2 * gain_rows + head_rows]
    grad_k_gain = gains[2 * gain_rows + head_rows :]
    grad_w_gate, grad_w_up = from_columns(grad_gate_up, [hidden, hidden])
    grad_w_query, grad_w_key, grad_w_value = from_columns(grad_qkv, [q_width, kv_width, kv_width])
    return (
        result,
        grad_x,
        grad_attn_gain,
        grad_w_query,
        grad_w_key,
        grad_w_value,
        grad_q_gain,
        grad_k_gain,
        grad_out_w.astype(F32),
        grad_mlp_gain,
        grad_w_gate,
        grad_w_up,
        grad_down.astype(F32),
    )


def solution(mesh):
    rows = P(("fsdp", "ctx"), None)
    vector = P(("fsdp", "ctx"))
    tokens = P("fsdp", "ctx", None)
    return jax.shard_map(
        per_device,
        mesh=mesh,
        in_specs=(
            tokens,
            P("fsdp"),
            P("fsdp"),
            P("fsdp", "ctx"),
            vector,
            rows,
            rows,
            rows,
            vector,
            vector,
            rows,
            vector,
            rows,
            rows,
            rows,
            tokens,
        ),
        out_specs=(
            tokens,
            tokens,
            vector,
            rows,
            rows,
            rows,
            vector,
            vector,
            rows,
            vector,
            rows,
            rows,
            rows,
        ),
        check_vma=False,
    )
```

```python
import functools

import jax
import jax.numpy as jnp
from jax import lax
from jax.experimental import pallas as pl
from jax.experimental.pallas import tpu as pltpu
from jax.sharding import PartitionSpec as P

H = 16
KVH = 8
HD = 128

EPS = 1e-06
THETA = 1000000.0
LOG2_E = 1.4426950408889634
BF = jnp.bfloat16
F32 = jnp.float32


def rms_scale(values, gain):
    inverse = lax.rsqrt(jnp.mean(values * values, axis=-1, keepdims=True) + EPS)
    return values * inverse * gain


def rope_tables(positions):
    freqs = THETA ** (-(jnp.arange(HD // 2, dtype=F32) * 2.0) / HD)
    angles = positions.astype(F32)[:, None] * freqs
    cosine = jnp.cos(angles)
    sine = jnp.sin(angles)
    return (jnp.concatenate([cosine, cosine], axis=-1), jnp.concatenate([-sine, sine], axis=-1))


def dot_nn(left, right):
    return lax.dot_general(left, right, (((1,), (0,)), ((), ())), preferred_element_type=F32)


def dot_nt(left, right):
    return lax.dot_general(left, right, (((1,), (1,)), ((), ())), preferred_element_type=F32)


def dot_tn(left, right):
    return lax.dot_general(left, right, (((0,), (0,)), ((), ())), preferred_element_type=F32)


def pick(stacked, index):
    return lax.dynamic_index_in_dim(stacked, index, 0, keepdims=False)


def xor_order(stacked, index):
    count = stacked.shape[0]
    bit = 1
    while bit < count:
        paired = stacked.reshape((count // (2 * bit), 2, bit) + stacked.shape[1:])
        flipped = jnp.concatenate([paired[:, 1:], paired[:, :1]], axis=1).reshape(stacked.shape)
        stacked = jnp.where((index & bit) != 0, flipped, stacked)
        bit *= 2
    return stacked


def key_block(kv_ref, block, blocks, cols):
    kc, kfb, kz = block // (2 * blocks), (block // blocks) % 2, block % blocks
    taken = kv_ref[kc, kfb, :, kz, :, cols]
    return taken.reshape(taken.shape[0] * taken.shape[1], taken.shape[2])


def stack_heads(ref, kv_head, per_key):
    parts = []
    for head in range(kv_head * per_key, (kv_head + 1) * per_key):
        part = ref[0, :, 0, :, head * HD : (head + 1) * HD]
        parts.append(part.reshape(part.shape[0] * part.shape[1], HD))
    return jnp.concatenate(parts, axis=0)


def attn_fwd_kernel(meta, q_ref, kv_ref, o_ref, lse_ref, acc_ref, total_ref, *, kv_heads, per_key, blocks, piece):
    tile_rows = q_ref.shape[1] * piece
    stacked = per_key * tile_rows
    kv_width = kv_heads * HD
    tile = pl.program_id(0)
    length, flip, start = meta[0], meta[1] * piece, meta[2 + tile]
    ids = 2 + 2 * blocks
    row = lax.broadcasted_iota(jnp.int32, (stacked, 1), 0) % tile_rows
    row_limit = jnp.minimum(start + (row ^ flip), length - 1)
    column = lax.broadcasted_iota(jnp.int32, (1, 2 * tile_rows), 1) ^ flip
    last = jnp.minimum(start, length - 1) // tile_rows
    acc_ref[...] = jnp.zeros_like(acc_ref)
    total_ref[...] = jnp.zeros_like(total_ref)
    queries = [stack_heads(q_ref, h, per_key) for h in range(kv_heads)]

    def body(step, carry):
        block_a, block_b = meta[ids + 2 * step], meta[ids + 2 * step + 1]
        allowed = step * (2 * tile_rows) + column <= row_limit
        for h in range(kv_heads):
            k_cols = slice(h * HD, (h + 1) * HD)
            v_cols = slice(kv_width + h * HD, kv_width + (h + 1) * HD)
            keys = jnp.concatenate([key_block(kv_ref, b, blocks, k_cols) for b in (block_a, block_b)], axis=0)
            values = jnp.concatenate([key_block(kv_ref, b, blocks, v_cols) for b in (block_a, block_b)], axis=0)
            scores = dot_nt(queries[h], keys)
            weight = jnp.where(allowed, jnp.exp2(scores * (HD ** (-0.5) * LOG2_E)), 0.0)
            part = weight[:, :HD]
            for at in range(HD, 2 * tile_rows, HD):
                part = part + weight[:, at : at + HD]
            total_ref[h] += part
            acc_ref[h] += dot_nn(weight.astype(BF), values)
        return carry

    lax.fori_loop(0, last // 2 + 1, body, 0)
    for h in range(kv_heads):
        total = jnp.sum(total_ref[h], axis=1, keepdims=True)
        out = (acc_ref[h] / total).astype(BF)
        for g in range(per_key):
            head = h * per_key + g
            o_ref[0, :, 0, :, head * HD : (head + 1) * HD] = out[g * tile_rows : (g + 1) * tile_rows].reshape(
                -1, piece, HD
            )
        lse_ref[0, h] = jnp.log2(jnp.sum(total_ref[h].T, axis=0, keepdims=True))


def attn_bwd_kernel(
    meta, q_ref, kv_ref, do_ref, o_ref, lse_ref, dq_ref, dkv_ref, sum_ref, dq_sum_ref, *, kv_heads, per_key, blocks, piece
):
    tile_rows = q_ref.shape[1] * piece
    stacked = per_key * tile_rows
    kv_width = kv_heads * HD
    tile = pl.program_id(0)
    length, flip, start = meta[0], meta[1] * piece, meta[2 + tile]
    ids = 2 + 2 * blocks
    row = lax.broadcasted_iota(jnp.int32, (1, stacked), 1) % tile_rows
    row_limit = jnp.minimum(start + (row ^ flip), length - 1)
    column = lax.broadcasted_iota(jnp.int32, (2 * tile_rows, 1), 0) ^ flip
    score_scale = HD ** (-0.5)

    @pl.when(tile == 0)
    def _():
        sum_ref[...] = jnp.zeros_like(sum_ref)

    dq_sum_ref[...] = jnp.zeros_like(dq_sum_ref)
    queries = [stack_heads(q_ref, h, per_key) for h in range(kv_heads)]
    grads = [stack_heads(do_ref, h, per_key) for h in range(kv_heads)]
    deltas = [
        jnp.sum((grads[h].astype(F32) * stack_heads(o_ref, h, per_key).astype(F32)).T, axis=0, keepdims=True)
        for h in range(kv_heads)
    ]
    logs = [lse_ref[0, h] for h in range(kv_heads)]

    def body(step, carry):
        pair = (meta[ids + 2 * step], meta[ids + 2 * step + 1])
        allowed = step * (2 * tile_rows) + column <= row_limit
        for h in range(kv_heads):
            k_cols = slice(h * HD, (h + 1) * HD)
            v_cols = slice(kv_width + h * HD, kv_width + (h + 1) * HD)
            keys = jnp.concatenate([key_block(kv_ref, b, blocks, k_cols) for b in pair], axis=0)
            values = jnp.concatenate([key_block(kv_ref, b, blocks, v_cols) for b in pair], axis=0)
            scores = dot_nt(keys, queries[h])
            probs = jnp.where(allowed, jnp.exp2(scores * (score_scale * LOG2_E) - logs[h]), 0.0)
            dprob = dot_nt(values, grads[h])
            dscore = (probs * (dprob - deltas[h])).astype(BF)
            dv = dot_nn(probs.astype(BF), grads[h])
            dk = dot_nn(dscore, queries[h])
            for n, block in enumerate(pair):
                sum_ref[block, :, k_cols] += dk[n * tile_rows : (n + 1) * tile_rows]
                sum_ref[block, :, v_cols] += dv[n * tile_rows : (n + 1) * tile_rows]
            dq_sum_ref[h] += dot_tn(dscore, keys)
        return carry

    lax.fori_loop(0, jnp.where(start < length, start // tile_rows // 2 + 1, 0), body, 0)
    for h in range(kv_heads):
        for g in range(per_key):
            head = h * per_key + g
            dq_ref[0, :, 0, :, head * HD : (head + 1) * HD] = (
                dq_sum_ref[h, g * tile_rows : (g + 1) * tile_rows] * score_scale
            ).reshape(-1, piece, HD)

    @pl.when(tile == pl.num_programs(0) - 1)
    def _():
        for kc in range(dkv_ref.shape[0]):
            for kfb in range(2):
                for kz in range(blocks):
                    block = (kc * 2 + kfb) * blocks + kz
                    dkv_ref[kc, kfb, :, kz, :, :kv_width] = (
                        (sum_ref[block, :, :kv_width] * score_scale).astype(BF).reshape(-1, piece, kv_width)
                    )
                    dkv_ref[kc, kfb, :, kz, :, kv_width:] = (
                        sum_ref[block, :, kv_width:].astype(BF).reshape(-1, piece, kv_width)
                    )


def attention_specs(queries, kv_all):
    halves, per_block, blocks, piece, q_width = queries.shape
    tile_spec = pl.BlockSpec((1, per_block, 1, piece, q_width), lambda t, meta: (t // blocks, 0, t % blocks, 0, 0))
    kv_spec = pl.BlockSpec(kv_all.shape, lambda t, meta: (0,) * 6)
    kv_heads = kv_all.shape[-1] // (2 * HD)
    per_key = q_width // HD // kv_heads
    lse_spec = pl.BlockSpec((1, kv_heads, 1, per_key * per_block * piece), lambda t, meta: (t, 0, 0, 0))
    sizes = dict(kv_heads=kv_heads, per_key=per_key, blocks=blocks, piece=piece)
    return halves * blocks, tile_spec, kv_spec, lse_spec, sizes, per_block * piece


def attention_forward(meta, queries, kv_all):
    tiles, tile_spec, kv_spec, lse_spec, sizes, tile_rows = attention_specs(queries, kv_all)
    kv_heads, per_key = sizes["kv_heads"], sizes["per_key"]
    stacked = per_key * tile_rows
    pairs = tiles * kv_heads * stacked * tiles * 2 * tile_rows // 2
    return pl.pallas_call(
        functools.partial(attn_fwd_kernel, **sizes),
        grid_spec=pltpu.PrefetchScalarGridSpec(
            num_scalar_prefetch=1,
            grid=(tiles,),
            in_specs=[tile_spec, kv_spec],
            out_specs=[tile_spec, lse_spec],
            scratch_shapes=[
                pltpu.VMEM((kv_heads, stacked, HD), F32),
                pltpu.VMEM((kv_heads, stacked, HD), F32),
            ],
        ),
        out_shape=[
            jax.ShapeDtypeStruct(queries.shape, BF),
            jax.ShapeDtypeStruct((tiles, kv_heads, 1, stacked), F32),
        ],
        cost_estimate=pl.CostEstimate(flops=pairs * HD * 4, transcendentals=pairs, bytes_accessed=4 * kv_all.size),
    )(meta, queries, kv_all)


def attention_backward(meta, queries, kv_all, dmix, mixture, logs):
    tiles, tile_spec, kv_spec, lse_spec, sizes, tile_rows = attention_specs(queries, kv_all)
    kv_heads, per_key = sizes["kv_heads"], sizes["per_key"]
    stacked = per_key * tile_rows
    key_blocks = kv_all.shape[0] * tiles
    pairs = tiles * kv_heads * stacked * tiles * 2 * tile_rows // 2
    return pl.pallas_call(
        functools.partial(attn_bwd_kernel, **sizes),
        grid_spec=pltpu.PrefetchScalarGridSpec(
            num_scalar_prefetch=1,
            grid=(tiles,),
            in_specs=[tile_spec, kv_spec, tile_spec, tile_spec, lse_spec],
            out_specs=[tile_spec, kv_spec],
            scratch_shapes=[
                pltpu.VMEM((key_blocks, tile_rows, kv_all.shape[-1]), F32),
                pltpu.VMEM((kv_heads, stacked, HD), F32),
            ],
        ),
        out_shape=[
            jax.ShapeDtypeStruct(queries.shape, F32),
            jax.ShapeDtypeStruct(kv_all.shape, BF),
        ],
        cost_estimate=pl.CostEstimate(flops=pairs * HD * 10, transcendentals=pairs, bytes_accessed=10 * kv_all.size),
    )(meta, queries, kv_all, dmix, mixture, logs)


def turned(values):
    return pltpu.roll(values, HD // 2, axis=1)


def project_kernel(
    x_ref, gain_ref, w_ref, cos_ref, sin_ref, q_gain_ref, k_gain_ref, normed_ref, proj_ref, q_ref, kv_ref, *, kv_width
):
    q_width = q_ref.shape[1]
    normed_ref[...] = rms_scale(x_ref[...].astype(F32), gain_ref[...]).astype(BF)
    proj = dot_nn(normed_ref[...], w_ref[...])
    proj_ref[...] = proj[:, : q_width + kv_width]
    cosine, sine = cos_ref[...], sin_ref[...]
    for at in range(0, q_width + kv_width, HD):
        gain = q_gain_ref[...] if at < q_width else k_gain_ref[...]
        normed = rms_scale(proj[:, at : at + HD], gain)
        rotated = (normed * cosine + turned(normed) * sine).astype(BF)
        if at < q_width:
            q_ref[:, at : at + HD] = rotated
        else:
            kv_ref[:, at - q_width : at - q_width + HD] = rotated
    kv_ref[:, kv_width:] = proj[:, q_width + kv_width :].astype(BF)


def project(x_all, attn_gain, w_qkv, cosine, sine, q_gain, k_gain, kv_width):
    tokens, width = x_all.shape
    columns = w_qkv.shape[1]
    q_width = columns - 2 * kv_width
    tile = min(256, tokens)

    def rows(n):
        return pl.BlockSpec((tile, n), lambda i: (i, 0))

    def whole(*shape):
        return pl.BlockSpec(shape, lambda i: (0, 0))

    return pl.pallas_call(
        functools.partial(project_kernel, kv_width=kv_width),
        grid=(tokens // tile,),
        in_specs=[rows(width), whole(1, width), whole(width, columns), rows(HD), rows(HD), whole(1, HD), whole(1, HD)],
        out_specs=[rows(width), rows(q_width + kv_width), rows(q_width), rows(2 * kv_width)],
        out_shape=[
            jax.ShapeDtypeStruct((tokens, width), BF),
            jax.ShapeDtypeStruct((tokens, q_width + kv_width), F32),
            jax.ShapeDtypeStruct((tokens, q_width), BF),
            jax.ShapeDtypeStruct((tokens, 2 * kv_width), BF),
        ],
        cost_estimate=pl.CostEstimate(
            flops=2 * tokens * width * columns, transcendentals=0, bytes_accessed=8 * tokens * width
        ),
    )(x_all, attn_gain[None], w_qkv, cosine, sine, q_gain[None], k_gain[None])


def unproject_kernel(
    dq_ref, dkv_ref, other_ref, proj_ref, cos_ref, sin_ref, q_gain_ref, k_gain_ref, dqkv_ref, dgain_ref, *, kv_width
):
    q_width = dq_ref.shape[1]

    @pl.when(pl.program_id(0) == 0)
    def _():
        dgain_ref[...] = jnp.zeros_like(dgain_ref)

    cosine, sine = cos_ref[...], sin_ref[...]
    dkv = dkv_ref[...].astype(F32) + other_ref[...].astype(F32)
    for at in range(0, q_width + kv_width, HD):
        is_q = at < q_width
        grad = dq_ref[:, at : at + HD] if is_q else dkv[:, at - q_width : at - q_width + HD]
        gain = q_gain_ref[...] if is_q else k_gain_ref[...]
        values = proj_ref[:, at : at + HD]
        inverse = lax.rsqrt(jnp.mean(values * values, axis=1, keepdims=True) + EPS)
        dnormed = grad * cosine + turned(grad * sine)
        n = 0 if is_q else 1
        dgain_ref[n : n + 1] += jnp.sum(dnormed * values * inverse, axis=0, keepdims=True)
        scaled = dnormed * gain
        inner = jnp.mean(scaled * values, axis=1, keepdims=True)
        dqkv_ref[:, at : at + HD] = (inverse * scaled - values * (inverse * inverse * inverse * inner)).astype(BF)
    dqkv_ref[:, q_width + kv_width :] = dkv[:, kv_width:].astype(BF)


def unproject(dq, dkv, other, proj, cosine, sine, q_gain, k_gain):
    tokens, q_width = dq.shape
    kv_width = dkv.shape[1] // 2
    columns = q_width + 2 * kv_width
    tile = min(256, tokens)

    def rows(n):
        return pl.BlockSpec((tile, n), lambda i: (i, 0))

    def whole(*shape):
        return pl.BlockSpec(shape, lambda i: (0, 0))

    return pl.pallas_call(
        functools.partial(unproject_kernel, kv_width=kv_width),
        grid=(tokens // tile,),
        in_specs=[
            rows(q_width),
            rows(2 * kv_width),
            rows(2 * kv_width),
            rows(q_width + kv_width),
            rows(HD),
            rows(HD),
            whole(1, HD),
            whole(1, HD),
        ],
        out_specs=[rows(columns), whole(2, HD)],
        out_shape=[jax.ShapeDtypeStruct((tokens, columns), BF), jax.ShapeDtypeStruct((2, HD), F32)],
        cost_estimate=pl.CostEstimate(
            flops=30 * tokens * columns, transcendentals=0, bytes_accessed=12 * tokens * columns
        ),
    )(dq, dkv, other, proj, cosine, sine, q_gain[None], k_gain[None])


def together(*values):
    return lax.optimization_barrier(values)


def per_device(
    layer_input,
    lengths,
    order,
    offsets,
    attn_gain,
    w_query,
    w_key,
    w_value,
    q_gain,
    k_gain,
    w_out,
    mlp_gain,
    w_gate,
    w_up,
    w_down,
    grad_out,
):
    groups, ring = lax.axis_size("fsdp"), lax.axis_size("ctx")
    _, rows, width = layer_input.shape
    lanes = ring // groups
    piece, block_rows = rows // groups, rows // 2
    per_block = block_rows // piece
    heads, kv_heads = H // groups, KVH // groups
    q_width, kv_width = heads * HD, kv_heads * HD
    shard_rows = w_query.shape[0]
    hidden = w_gate.shape[1] // groups
    own = lax.axis_index("fsdp")
    own_ctx = lax.axis_index("ctx")
    plane, lane = own_ctx // lanes, own_ctx % lanes
    steps = range(groups)
    tokens = groups * rows

    def swap(block, step):
        if step == 0:
            return block
        return lax.ppermute(block, "fsdp", [(i, i ^ step) for i in range(groups)])

    def swap_plane(block, step):
        if step == 0:
            return block
        return lax.ppermute(block, "ctx", [(i, (i // lanes ^ step) * lanes + i % lanes) for i in range(ring)])

    def swap_lane(block, step):
        if step == 0:
            return block
        return lax.ppermute(block, "ctx", [(i, i // lanes * lanes + (i % lanes ^ step)) for i in range(ring)])

    def gather_all(part):
        for axis, index, count in (("ctx", own_ctx, ring), ("fsdp", own, groups)):
            step = 1
            while step < count:
                other = lax.ppermute(part, axis, [(i, i ^ step) for i in range(count)])
                low = (index & step) == 0
                part = jnp.concatenate([jnp.where(low, part, other), jnp.where(low, other, part)], axis=0)
                step *= 2
        return part

    def scatter_all(part):
        for axis, index, count in (("fsdp", own, groups), ("ctx", own_ctx, ring)):
            step = count // 2
            while step:
                half = part.shape[0] // 2
                low = (index & step) == 0
                kept = jnp.where(low, part[:half], part[half:])
                sent = jnp.where(low, part[half:], part[:half])
                part = kept + lax.ppermute(sent, axis, [(i, i ^ step) for i in range(count)])
                step //= 2
        return part

    def to_pieces(local):
        pieces = local.reshape(groups, piece, width)
        return jnp.stack([swap(pick(pieces, own ^ k), k) for k in steps])

    def to_plane(spread, holder):
        mine = [swap_plane(pick(spread, own ^ holder[plane ^ k]), k) for k in steps]
        return jnp.concatenate(mine, axis=0)

    def leave_plane(mine):
        return jnp.stack([swap_plane(mine[k], k) for k in steps])

    def from_plane(spread, held):
        back = jnp.stack([swap(pick(spread, plane ^ held[own ^ k]), k) for k in steps])
        return xor_order(back, own).reshape(1, rows, width)

    small = jnp.concatenate(
        [
            attn_gain.astype(F32),
            mlp_gain.astype(F32),
            q_gain.astype(F32),
            k_gain.astype(F32),
            lengths.astype(F32),
            order.astype(F32),
            offsets.reshape(-1).astype(F32),
        ]
    )[None, :]
    small_all = gather_all(small)
    spread, w_query, w_key, w_value = together(to_pieces(layer_input[0]), w_query, w_key, w_value)
    x_own = to_plane(spread, jnp.arange(groups, dtype=jnp.int32))
    x_own, small_all = together(x_own, small_all)
    gain_rows, head_rows = attn_gain.shape[0], q_gain.shape[0]
    at = 0
    attn_gain_full = small_all[:, at : at + gain_rows].reshape(-1)
    at += gain_rows
    mlp_gain_full = small_all[:, at : at + gain_rows].reshape(-1)
    at += gain_rows
    q_gain_full = small_all[:, at : at + head_rows].reshape(-1)
    at += head_rows
    k_gain_full = small_all[:, at : at + head_rows].reshape(-1)
    at += head_rows
    whole = small_all[:, at:].astype(jnp.int32).reshape(groups, ring, 4)
    lengths_all = whole[:, 0, 0]
    order_all = whole[:, 0, 1]
    each = jnp.arange(groups, dtype=jnp.int32)
    slot_of = jnp.sum(jnp.where(order_all[None, :] == each[:, None], each[None, :], 0), axis=1)
    length = pick(lengths_all, plane)
    starts = pick(whole[:, :, 2:4], plane).reshape(groups, lanes, 2)
    starts = jnp.transpose(xor_order(starts, plane), (1, 2, 0))
    starts = jnp.transpose(xor_order(starts, lane), (1, 0, 2))
    starts = jnp.transpose(xor_order(starts, own // per_block), (1, 0, 2))
    flip = own % per_block
    tile_starts = starts[0].reshape(-1)
    block_starts = starts.reshape(-1)
    block_ids = jnp.arange(block_starts.shape[0], dtype=jnp.int32)
    block_at = jnp.sum(
        jnp.where(block_starts[None, :] == (block_ids * block_rows)[:, None], block_ids[None, :], 0), axis=1
    )
    meta = jnp.concatenate([length[None], flip[None].astype(jnp.int32), tile_starts, block_at])
    within = jnp.arange(block_rows, dtype=jnp.int32) ^ (flip * piece)
    positions = (
        starts[0][:, None, :, None] + within.reshape(1, per_block, 1, piece)
    ).reshape(groups, rows)
    valid_own = positions[0] < length

    def to_columns(parts):
        out = jnp.zeros((groups, shard_rows, sum(p.shape[1] for p in parts) // groups), BF)
        for k in steps:
            piece_k = jnp.concatenate(
                [
                    lax.dynamic_slice_in_dim(p, (own ^ k) * (p.shape[1] // groups), p.shape[1] // groups, 1)
                    for p in parts
                ],
                axis=1,
            )
            out = lax.dynamic_update_index_in_dim(out, swap(piece_k, k), own ^ k, 0)
        return out

    def from_columns(grad, widths):
        outs = [jnp.zeros((shard_rows, w * groups), F32) for w in widths]
        for k in steps:
            piece_k = swap(pick(grad, own ^ k), k).astype(F32)
            at = 0
            for n, w in enumerate(widths):
                outs[n] = lax.dynamic_update_slice_in_dim(outs[n], piece_k[:, at : at + w], (own ^ k) * w, 1)
                at += w
        return outs

    qkv_local = to_columns([w_query, w_key, w_value])
    qkv_local, x_own = together(qkv_local, x_own)
    w_qkv = lax.all_gather(qkv_local, "ctx", axis=1, tiled=True).reshape(width, -1)
    w_out_full = lax.all_gather(w_out, "ctx", axis=0, tiled=True)
    x_all = jnp.concatenate([swap(x_own, k) for k in steps], axis=0)
    cosine, sine = rope_tables(positions.reshape(-1))
    normed_one, proj, query_rot, kv_rot = project(
        x_all, attn_gain_full, w_qkv, cosine, sine, q_gain_full, k_gain_full, kv_width
    )
    w_gate, w_up, grad_out, normed_one = together(w_gate, w_up, grad_out, normed_one)
    gate_up_local = to_columns([w_gate, w_up])
    w_gate_up = lax.all_gather(gate_up_local, "ctx", axis=1, tiled=True).reshape(width, -1)
    w_down_full = lax.all_gather(w_down, "ctx", axis=0, tiled=True)
    tile_shape = (2, per_block, groups, piece, -1)
    queries = query_rot.reshape(tile_shape)
    kv_own = kv_rot.reshape(tile_shape)
    kv_all = jnp.stack([swap_lane(kv_own, k) for k in range(lanes)])
    mixture, logs = attention_forward(meta, queries, kv_all)
    mix_b = mixture.reshape(tokens, -1)
    attn_part = dot_nn(mix_b, w_out_full).reshape(groups, rows, width)
    hidden_res = x_own.astype(F32) + attn_part[0]
    for k in steps[1:]:
        hidden_res = hidden_res + swap(attn_part[k].astype(BF), k).astype(F32)
    normed_two_own = rms_scale(hidden_res, mlp_gain_full).astype(BF)
    normed_two = jnp.concatenate([swap(normed_two_own, k) for k in steps], axis=0)
    dy_own = to_plane(to_pieces(grad_out[0]), slot_of)
    dy_own = jnp.where(valid_own[:, None], dy_own, jnp.zeros((), BF))
    gate_up, dy_own = together(dot_nn(normed_two, w_gate_up), dy_own)
    gate_proj, up_proj = gate_up[:, :hidden], gate_up[:, hidden:]
    hidden_act = (jax.nn.silu(gate_proj) * up_proj).astype(BF)

    dy_b = jnp.concatenate([swap(dy_own, k) for k in steps], axis=0)
    grad_down_part, dy_after = together(dot_tn(hidden_act, dy_b).astype(BF), dy_b)
    grad_down = lax.psum_scatter(grad_down_part, "ctx", scatter_dimension=0, tiled=True)
    dhid = dot_nt(dy_after, w_down_full)
    _, swiglu_pull = jax.vjp(lambda g, u: jax.nn.silu(g) * u, gate_proj, up_proj)
    dgate_f, dup_f = swiglu_pull(dhid)
    dgate, dup = dgate_f.astype(BF), dup_f.astype(BF)
    dn_two_part = dot_nt(jnp.concatenate([dgate, dup], axis=1), w_gate_up).reshape(groups, rows, width)
    dn_two_part, normed_two = together(dn_two_part, normed_two)
    dn_two = dn_two_part[0]
    for k in steps[1:]:
        dn_two = dn_two + swap(dn_two_part[k].astype(BF), k).astype(F32)
    grad_gate = lax.psum_scatter(
        dot_tn(normed_two, dgate).astype(BF).reshape(groups, -1, hidden), "ctx", scatter_dimension=1, tiled=True
    )
    grad_up = lax.psum_scatter(
        dot_tn(normed_two, dup).astype(BF).reshape(groups, -1, hidden), "ctx", scatter_dimension=1, tiled=True
    )
    dn_two, grad_down = together(dn_two, grad_down)
    _, norm_two_pull = jax.vjp(rms_scale, hidden_res, mlp_gain_full)
    dh_norm, dmlp_gain_part = norm_two_pull(dn_two)
    dh_rows = dy_own.astype(F32) + dh_norm
    dattn_own = dh_rows.astype(BF)
    dattn_b = jnp.concatenate([swap(dattn_own, k) for k in steps], axis=0)
    out_part = dot_nn(hidden_act, w_down_full).reshape(groups, rows, width)
    out_sent = [out_part[k].astype(BF) for k in steps[1:]]
    dattn_b, grad_gate = together(dattn_b, grad_gate)
    dmix_b = dot_nt(dattn_b, w_out_full).astype(BF)
    dmix_b, grad_out_part, *out_sent = together(dmix_b, dot_tn(mix_b, dattn_b).astype(BF), *out_sent)
    grad_out_w = lax.psum_scatter(grad_out_part, "ctx", scatter_dimension=0, tiled=True)

    dq_rot, dkv_parts = attention_backward(meta, queries, kv_all, dmix_b.reshape(queries.shape), mixture, logs)
    result, dq_rot = together(out_part[0] + hidden_res, dq_rot)
    for k in steps[1:]:
        result = result + swap(out_sent[k - 1], k).astype(F32)
    result = result.astype(BF)
    dkv_parts = dkv_parts.reshape(lanes, tokens, -1)
    other = swap_lane(dkv_parts[1], 1)
    for k in range(2, lanes):
        other = other + swap_lane(dkv_parts[k], k)
    dqkv, dhead_gains = unproject(
        dq_rot.reshape(tokens, -1), dkv_parts[0], other, proj, cosine, sine, q_gain_full, k_gain_full
    )

    dqkv, grad_up, result = together(dqkv, grad_up, result)
    grad_qkv_part = dot_tn(normed_one, dqkv).astype(BF).reshape(groups, -1, dqkv.shape[1])
    grad_qkv = lax.psum_scatter(grad_qkv_part, "ctx", scatter_dimension=1, tiled=True)
    dn_one_part = dot_nt(dqkv, w_qkv).reshape(groups, rows, width)
    dn_one = dn_one_part[0]
    for k in steps[1:]:
        dn_one = dn_one + swap(dn_one_part[k].astype(BF), k).astype(F32)
    result = leave_plane(result.reshape(groups, piece, width))
    dn_one, grad_out_w, result = together(dn_one, grad_out_w, result)
    result = from_plane(result, order_all)
    _, norm_one_pull = jax.vjp(rms_scale, x_own.astype(F32), attn_gain_full)
    dflat_norm, dattn_gain_part = norm_one_pull(dn_one)
    spread = leave_plane((dh_rows + dflat_norm).astype(BF).reshape(groups, piece, width))
    grad_w_query, grad_w_key, grad_w_value = from_columns(grad_qkv, [q_width, kv_width, kv_width])
    spread, grad_w_query = together(spread, grad_w_query)
    grad_x = from_plane(spread, each)

    devices = groups * ring
    gains = jnp.concatenate(
        [
            dattn_gain_part.reshape(devices, -1),
            dmlp_gain_part.reshape(devices, -1),
            dhead_gains[0].reshape(devices, -1),
            dhead_gains[1].reshape(devices, -1),
        ],
        axis=1,
    )
    gains = scatter_all(gains)[0]
    grad_attn_gain = gains[:gain_rows]
    grad_mlp_gain = gains[gain_rows : 2 * gain_rows]
    grad_q_gain = gains[2 * gain_rows : 2 * gain_rows + head_rows]
    grad_k_gain = gains[2 * gain_rows + head_rows :]
    (grad_w_gate,) = from_columns(grad_gate, [hidden])
    (grad_w_up,) = from_columns(grad_up, [hidden])
    return (
        result,
        grad_x,
        grad_attn_gain,
        grad_w_query,
        grad_w_key,
        grad_w_value,
        grad_q_gain,
        grad_k_gain,
        grad_out_w.astype(F32),
        grad_mlp_gain,
        grad_w_gate,
        grad_w_up,
        grad_down.astype(F32),
    )


def solution(mesh):
    rows = P(("fsdp", "ctx"), None)
    vector = P(("fsdp", "ctx"))
    tokens = P("fsdp", "ctx", None)
    return jax.shard_map(
        per_device,
        mesh=mesh,
        in_specs=(
            tokens,
            P("fsdp"),
            P("fsdp"),
            P("fsdp", "ctx"),
            vector,
            rows,
            rows,
            rows,
            vector,
            vector,
            rows,
            vector,
            rows,
            rows,
            rows,
            tokens,
        ),
        out_specs=(
            tokens,
            tokens,
            vector,
            rows,
            rows,
            rows,
            vector,
            vector,
            rows,
            vector,
            rows,
            rows,
            rows,
        ),
        check_vma=False,
    )
```

```python
import functools

import jax
import jax.numpy as jnp
from jax import lax
from jax.experimental import pallas as pl
from jax.experimental.pallas import tpu as pltpu
from jax.sharding import PartitionSpec as P

H = 16
KVH = 8
HD = 128

EPS = 1e-06
THETA = 1000000.0
LOG2_E = 1.4426950408889634
STEP = 4
BF = jnp.bfloat16
F32 = jnp.float32


def rms_scale(values, gain):
    inverse = lax.rsqrt(jnp.mean(values * values, axis=-1, keepdims=True) + EPS)
    return values * inverse * gain


def rope_tables(positions):
    freqs = THETA ** (-(jnp.arange(HD // 2, dtype=F32) * 2.0) / HD)
    angles = positions.astype(F32)[:, None] * freqs
    cosine = jnp.cos(angles)
    sine = jnp.sin(angles)
    return (jnp.concatenate([cosine, cosine], axis=-1), jnp.concatenate([-sine, sine], axis=-1))


def dot_nn(left, right):
    return lax.dot_general(left, right, (((1,), (0,)), ((), ())), preferred_element_type=F32)


def dot_nt(left, right):
    return lax.dot_general(left, right, (((1,), (1,)), ((), ())), preferred_element_type=F32)


def dot_tn(left, right):
    return lax.dot_general(left, right, (((0,), (0,)), ((), ())), preferred_element_type=F32)


def pick(stacked, index):
    return lax.dynamic_index_in_dim(stacked, index, 0, keepdims=False)


def xor_order(stacked, index):
    count = stacked.shape[0]
    bit = 1
    while bit < count:
        paired = stacked.reshape((count // (2 * bit), 2, bit) + stacked.shape[1:])
        flipped = jnp.concatenate([paired[:, 1:], paired[:, :1]], axis=1).reshape(stacked.shape)
        stacked = jnp.where((index & bit) != 0, flipped, stacked)
        bit *= 2
    return stacked


def key_block(kv_ref, block, blocks, cols):
    kc, kfb, kz = block // (2 * blocks), (block // blocks) % 2, block % blocks
    taken = kv_ref[kc, kfb, :, kz, :, cols]
    return taken.reshape(taken.shape[0] * taken.shape[1], taken.shape[2])


def stack_heads(ref, kv_head, per_key):
    parts = []
    for head in range(kv_head * per_key, (kv_head + 1) * per_key):
        part = ref[0, :, 0, :, head * HD : (head + 1) * HD]
        parts.append(part.reshape(part.shape[0] * part.shape[1], HD))
    return jnp.concatenate(parts, axis=0)


def attn_fwd_kernel(meta, q_ref, kv_ref, o_ref, lse_ref, acc_ref, total_ref, *, kv_heads, per_key, blocks, piece):
    tile_rows = q_ref.shape[1] * piece
    stacked = per_key * tile_rows
    kv_width = kv_heads * HD
    tile = pl.program_id(0)
    length, flip, start = meta[0], meta[1] * piece, meta[2 + tile]
    ids = 2 + 2 * blocks
    row = lax.broadcasted_iota(jnp.int32, (stacked, 1), 0) % tile_rows
    row_limit = jnp.minimum(start + (row ^ flip), length - 1)
    column = lax.broadcasted_iota(jnp.int32, (1, STEP * tile_rows), 1) ^ flip
    last = jnp.minimum(start, length - 1) // tile_rows
    acc_ref[...] = jnp.zeros_like(acc_ref)
    total_ref[...] = jnp.zeros_like(total_ref)
    queries = [stack_heads(q_ref, h, per_key) for h in range(kv_heads)]

    def body(step, carry):
        taken = [meta[ids + STEP * step + n] for n in range(STEP)]
        allowed = step * (STEP * tile_rows) + column <= row_limit

        def columns_of(at):
            return jnp.concatenate([key_block(kv_ref, b, blocks, slice(at, at + HD)) for b in taken], axis=0)

        scores = [dot_nt(queries[h], columns_of(h * HD)) for h in range(kv_heads)]
        weights = [jnp.where(allowed, jnp.exp2(x * (HD ** (-0.5) * LOG2_E)), 0.0) for x in scores]
        parts = [dot_nn(weights[h].astype(BF), columns_of(kv_width + h * HD)) for h in range(kv_heads)]
        for h in range(kv_heads):
            part = weights[h][:, :HD]
            for at in range(HD, STEP * tile_rows, HD):
                part = part + weights[h][:, at : at + HD]
            total_ref[h] += part
            acc_ref[h] += parts[h]
        return carry

    lax.fori_loop(0, last // STEP + 1, body, 0)
    for h in range(kv_heads):
        total = jnp.sum(total_ref[h], axis=1, keepdims=True)
        out = (acc_ref[h] / total).astype(BF)
        for g in range(per_key):
            head = h * per_key + g
            o_ref[0, :, 0, :, head * HD : (head + 1) * HD] = out[g * tile_rows : (g + 1) * tile_rows].reshape(
                -1, piece, HD
            )
        lse_ref[0, h] = jnp.log2(jnp.sum(total_ref[h].T, axis=0, keepdims=True))


def attn_bwd_kernel(
    meta, q_ref, kv_ref, do_ref, o_ref, lse_ref, dq_ref, dkv_ref, sum_ref, dq_sum_ref, *, kv_heads, per_key, blocks, piece
):
    tile_rows = q_ref.shape[1] * piece
    stacked = per_key * tile_rows
    kv_width = kv_heads * HD
    tile = pl.program_id(0)
    length, flip, start = meta[0], meta[1] * piece, meta[2 + tile]
    ids = 2 + 2 * blocks
    row = lax.broadcasted_iota(jnp.int32, (1, stacked), 1) % tile_rows
    row_limit = jnp.minimum(start + (row ^ flip), length - 1)
    column = lax.broadcasted_iota(jnp.int32, (STEP * tile_rows, 1), 0) ^ flip
    score_scale = HD ** (-0.5)

    @pl.when(tile == 0)
    def _():
        sum_ref[...] = jnp.zeros_like(sum_ref)

    dq_sum_ref[...] = jnp.zeros_like(dq_sum_ref)
    queries = [stack_heads(q_ref, h, per_key) for h in range(kv_heads)]
    grads = [stack_heads(do_ref, h, per_key) for h in range(kv_heads)]
    deltas = [
        jnp.sum((grads[h].astype(F32) * stack_heads(o_ref, h, per_key).astype(F32)).T, axis=0, keepdims=True)
        for h in range(kv_heads)
    ]
    logs = [lse_ref[0, h] for h in range(kv_heads)]

    def body(step, carry):
        taken = [meta[ids + STEP * step + n] for n in range(STEP)]
        allowed = step * (STEP * tile_rows) + column <= row_limit

        def columns_of(at):
            return jnp.concatenate([key_block(kv_ref, b, blocks, slice(at, at + HD)) for b in taken], axis=0)

        each = range(kv_heads)
        keys = [columns_of(h * HD) for h in each]
        scores = [dot_nt(keys[h], queries[h]) for h in each]
        dprobs = [dot_nt(columns_of(kv_width + h * HD), grads[h]) for h in each]
        probs = [
            jnp.where(allowed, jnp.exp2(scores[h] * (score_scale * LOG2_E) - logs[h]), 0.0) for h in each
        ]
        dscores = [(probs[h] * (dprobs[h] - deltas[h])).astype(BF) for h in each]
        dvs = [dot_nn(probs[h].astype(BF), grads[h]) for h in each]
        dks = [dot_nn(dscores[h], queries[h]) for h in each]
        dqs = [dot_tn(dscores[h], keys[h]) for h in each]
        for h in each:
            dq_sum_ref[h] += dqs[h]
            for n, block in enumerate(taken):
                part = slice(n * tile_rows, (n + 1) * tile_rows)
                sum_ref[block, :, h * HD : (h + 1) * HD] += dks[h][part]
                sum_ref[block, :, kv_width + h * HD : kv_width + (h + 1) * HD] += dvs[h][part]
        return carry

    lax.fori_loop(0, jnp.where(start < length, start // tile_rows // STEP + 1, 0), body, 0)
    for h in range(kv_heads):
        for g in range(per_key):
            head = h * per_key + g
            dq_ref[0, :, 0, :, head * HD : (head + 1) * HD] = (
                dq_sum_ref[h, g * tile_rows : (g + 1) * tile_rows] * score_scale
            ).reshape(-1, piece, HD)

    @pl.when(tile == pl.num_programs(0) - 1)
    def _():
        for kc in range(dkv_ref.shape[0]):
            for kfb in range(2):
                for kz in range(blocks):
                    block = (kc * 2 + kfb) * blocks + kz
                    dkv_ref[kc, kfb, :, kz, :, :kv_width] = (
                        (sum_ref[block, :, :kv_width] * score_scale).astype(BF).reshape(-1, piece, kv_width)
                    )
                    dkv_ref[kc, kfb, :, kz, :, kv_width:] = (
                        sum_ref[block, :, kv_width:].astype(BF).reshape(-1, piece, kv_width)
                    )


def attention_specs(queries, kv_all):
    halves, per_block, blocks, piece, q_width = queries.shape
    tile_spec = pl.BlockSpec((1, per_block, 1, piece, q_width), lambda t, meta: (t // blocks, 0, t % blocks, 0, 0))
    kv_spec = pl.BlockSpec(kv_all.shape, lambda t, meta: (0,) * 6)
    kv_heads = kv_all.shape[-1] // (2 * HD)
    per_key = q_width // HD // kv_heads
    lse_spec = pl.BlockSpec((1, kv_heads, 1, per_key * per_block * piece), lambda t, meta: (t, 0, 0, 0))
    sizes = dict(kv_heads=kv_heads, per_key=per_key, blocks=blocks, piece=piece)
    return halves * blocks, tile_spec, kv_spec, lse_spec, sizes, per_block * piece


def attention_forward(meta, queries, kv_all):
    tiles, tile_spec, kv_spec, lse_spec, sizes, tile_rows = attention_specs(queries, kv_all)
    kv_heads, per_key = sizes["kv_heads"], sizes["per_key"]
    stacked = per_key * tile_rows
    pairs = tiles * kv_heads * stacked * tiles * 2 * tile_rows // 2
    return pl.pallas_call(
        functools.partial(attn_fwd_kernel, **sizes),
        grid_spec=pltpu.PrefetchScalarGridSpec(
            num_scalar_prefetch=1,
            grid=(tiles,),
            in_specs=[tile_spec, kv_spec],
            out_specs=[tile_spec, lse_spec],
            scratch_shapes=[
                pltpu.VMEM((kv_heads, stacked, HD), F32),
                pltpu.VMEM((kv_heads, stacked, HD), F32),
            ],
        ),
        out_shape=[
            jax.ShapeDtypeStruct(queries.shape, BF),
            jax.ShapeDtypeStruct((tiles, kv_heads, 1, stacked), F32),
        ],
        cost_estimate=pl.CostEstimate(flops=pairs * HD * 4, transcendentals=pairs, bytes_accessed=4 * kv_all.size),
    )(meta, queries, kv_all)


def attention_backward(meta, queries, kv_all, dmix, mixture, logs):
    tiles, tile_spec, kv_spec, lse_spec, sizes, tile_rows = attention_specs(queries, kv_all)
    kv_heads, per_key = sizes["kv_heads"], sizes["per_key"]
    stacked = per_key * tile_rows
    key_blocks = kv_all.shape[0] * tiles
    pairs = tiles * kv_heads * stacked * tiles * 2 * tile_rows // 2
    return pl.pallas_call(
        functools.partial(attn_bwd_kernel, **sizes),
        grid_spec=pltpu.PrefetchScalarGridSpec(
            num_scalar_prefetch=1,
            grid=(tiles,),
            in_specs=[tile_spec, kv_spec, tile_spec, tile_spec, lse_spec],
            out_specs=[tile_spec, kv_spec],
            scratch_shapes=[
                pltpu.VMEM((key_blocks, tile_rows, kv_all.shape[-1]), F32),
                pltpu.VMEM((kv_heads, stacked, HD), F32),
            ],
        ),
        out_shape=[
            jax.ShapeDtypeStruct(queries.shape, F32),
            jax.ShapeDtypeStruct(kv_all.shape, BF),
        ],
        cost_estimate=pl.CostEstimate(flops=pairs * HD * 10, transcendentals=pairs, bytes_accessed=10 * kv_all.size),
    )(meta, queries, kv_all, dmix, mixture, logs)


def turned(values):
    return pltpu.roll(values, HD // 2, axis=1)


def project_kernel(
    x_ref, gain_ref, w_ref, cos_ref, sin_ref, q_gain_ref, k_gain_ref, normed_ref, proj_ref, q_ref, kv_ref, *, kv_width
):
    q_width = q_ref.shape[1]
    normed_ref[...] = rms_scale(x_ref[...].astype(F32), gain_ref[...]).astype(BF)
    proj = dot_nn(normed_ref[...], w_ref[...])
    proj_ref[...] = proj[:, : q_width + kv_width]
    cosine, sine = cos_ref[...], sin_ref[...]
    for at in range(0, q_width + kv_width, HD):
        gain = q_gain_ref[...] if at < q_width else k_gain_ref[...]
        normed = rms_scale(proj[:, at : at + HD], gain)
        rotated = (normed * cosine + turned(normed) * sine).astype(BF)
        if at < q_width:
            q_ref[:, at : at + HD] = rotated
        else:
            kv_ref[:, at - q_width : at - q_width + HD] = rotated
    kv_ref[:, kv_width:] = proj[:, q_width + kv_width :].astype(BF)


def project(x_all, attn_gain, w_qkv, cosine, sine, q_gain, k_gain, kv_width):
    tokens, width = x_all.shape
    columns = w_qkv.shape[1]
    q_width = columns - 2 * kv_width
    tile = min(256, tokens)

    def rows(n):
        return pl.BlockSpec((tile, n), lambda i: (i, 0))

    def whole(*shape):
        return pl.BlockSpec(shape, lambda i: (0, 0))

    return pl.pallas_call(
        functools.partial(project_kernel, kv_width=kv_width),
        grid=(tokens // tile,),
        in_specs=[rows(width), whole(1, width), whole(width, columns), rows(HD), rows(HD), whole(1, HD), whole(1, HD)],
        out_specs=[rows(width), rows(q_width + kv_width), rows(q_width), rows(2 * kv_width)],
        out_shape=[
            jax.ShapeDtypeStruct((tokens, width), BF),
            jax.ShapeDtypeStruct((tokens, q_width + kv_width), F32),
            jax.ShapeDtypeStruct((tokens, q_width), BF),
            jax.ShapeDtypeStruct((tokens, 2 * kv_width), BF),
        ],
        cost_estimate=pl.CostEstimate(
            flops=2 * tokens * width * columns, transcendentals=0, bytes_accessed=8 * tokens * width
        ),
    )(x_all, attn_gain[None], w_qkv, cosine, sine, q_gain[None], k_gain[None])


def unproject_kernel(
    dq_ref, dkv_ref, other_ref, proj_ref, cos_ref, sin_ref, q_gain_ref, k_gain_ref, dqkv_ref, dgain_ref, *, kv_width
):
    q_width = dq_ref.shape[1]

    @pl.when(pl.program_id(0) == 0)
    def _():
        dgain_ref[...] = jnp.zeros_like(dgain_ref)

    cosine, sine = cos_ref[...], sin_ref[...]
    dkv = dkv_ref[...].astype(F32) + other_ref[...].astype(F32)
    for at in range(0, q_width + kv_width, HD):
        is_q = at < q_width
        grad = dq_ref[:, at : at + HD] if is_q else dkv[:, at - q_width : at - q_width + HD]
        gain = q_gain_ref[...] if is_q else k_gain_ref[...]
        values = proj_ref[:, at : at + HD]
        inverse = lax.rsqrt(jnp.mean(values * values, axis=1, keepdims=True) + EPS)
        dnormed = grad * cosine + turned(grad * sine)
        n = 0 if is_q else 1
        dgain_ref[n : n + 1] += jnp.sum(dnormed * values * inverse, axis=0, keepdims=True)
        scaled = dnormed * gain
        inner = jnp.mean(scaled * values, axis=1, keepdims=True)
        dqkv_ref[:, at : at + HD] = (inverse * scaled - values * (inverse * inverse * inverse * inner)).astype(BF)
    dqkv_ref[:, q_width + kv_width :] = dkv[:, kv_width:].astype(BF)


def unproject(dq, dkv, other, proj, cosine, sine, q_gain, k_gain):
    tokens, q_width = dq.shape
    kv_width = dkv.shape[1] // 2
    columns = q_width + 2 * kv_width
    tile = min(256, tokens)

    def rows(n):
        return pl.BlockSpec((tile, n), lambda i: (i, 0))

    def whole(*shape):
        return pl.BlockSpec(shape, lambda i: (0, 0))

    return pl.pallas_call(
        functools.partial(unproject_kernel, kv_width=kv_width),
        grid=(tokens // tile,),
        in_specs=[
            rows(q_width),
            rows(2 * kv_width),
            rows(2 * kv_width),
            rows(q_width + kv_width),
            rows(HD),
            rows(HD),
            whole(1, HD),
            whole(1, HD),
        ],
        out_specs=[rows(columns), whole(2, HD)],
        out_shape=[jax.ShapeDtypeStruct((tokens, columns), BF), jax.ShapeDtypeStruct((2, HD), F32)],
        cost_estimate=pl.CostEstimate(
            flops=30 * tokens * columns, transcendentals=0, bytes_accessed=12 * tokens * columns
        ),
    )(dq, dkv, other, proj, cosine, sine, q_gain[None], k_gain[None])


def together(*values):
    return lax.optimization_barrier(values)


def per_device(
    layer_input,
    lengths,
    order,
    offsets,
    attn_gain,
    w_query,
    w_key,
    w_value,
    q_gain,
    k_gain,
    w_out,
    mlp_gain,
    w_gate,
    w_up,
    w_down,
    grad_out,
):
    groups, ring = lax.axis_size("fsdp"), lax.axis_size("ctx")
    _, rows, width = layer_input.shape
    lanes = ring // groups
    piece, block_rows = rows // groups, rows // 2
    per_block = block_rows // piece
    heads, kv_heads = H // groups, KVH // groups
    q_width, kv_width = heads * HD, kv_heads * HD
    shard_rows = w_query.shape[0]
    hidden = w_gate.shape[1] // groups
    own = lax.axis_index("fsdp")
    own_ctx = lax.axis_index("ctx")
    plane, lane = own_ctx // lanes, own_ctx % lanes
    steps = range(groups)
    tokens = groups * rows

    def swap(block, step):
        if step == 0:
            return block
        return lax.ppermute(block, "fsdp", [(i, i ^ step) for i in range(groups)])

    def swap_plane(block, step):
        if step == 0:
            return block
        return lax.ppermute(block, "ctx", [(i, (i // lanes ^ step) * lanes + i % lanes) for i in range(ring)])

    def swap_lane(block, step):
        if step == 0:
            return block
        return lax.ppermute(block, "ctx", [(i, i // lanes * lanes + (i % lanes ^ step)) for i in range(ring)])

    def gather_all(part):
        for axis, index, count in (("ctx", own_ctx, ring), ("fsdp", own, groups)):
            step = 1
            while step < count:
                other = lax.ppermute(part, axis, [(i, i ^ step) for i in range(count)])
                low = (index & step) == 0
                part = jnp.concatenate([jnp.where(low, part, other), jnp.where(low, other, part)], axis=0)
                step *= 2
        return part

    def scatter_all(part):
        for axis, index, count in (("fsdp", own, groups), ("ctx", own_ctx, ring)):
            step = count // 2
            while step:
                half = part.shape[0] // 2
                low = (index & step) == 0
                kept = jnp.where(low, part[:half], part[half:])
                sent = jnp.where(low, part[half:], part[:half])
                part = kept + lax.ppermute(sent, axis, [(i, i ^ step) for i in range(count)])
                step //= 2
        return part

    def to_pieces(local):
        pieces = local.reshape(groups, piece, width)
        return jnp.stack([swap(pick(pieces, own ^ k), k) for k in steps])

    def to_plane(spread, holder):
        mine = [swap_plane(pick(spread, own ^ holder[plane ^ k]), k) for k in steps]
        return jnp.concatenate(mine, axis=0)

    def leave_plane(mine):
        return jnp.stack([swap_plane(mine[k], k) for k in steps])

    def from_plane(spread, held):
        back = jnp.stack([swap(pick(spread, plane ^ held[own ^ k]), k) for k in steps])
        return xor_order(back, own).reshape(1, rows, width)

    small = jnp.concatenate(
        [
            attn_gain.astype(F32),
            mlp_gain.astype(F32),
            q_gain.astype(F32),
            k_gain.astype(F32),
            lengths.astype(F32),
            order.astype(F32),
            offsets.reshape(-1).astype(F32),
        ]
    )[None, :]
    small_all = gather_all(small)
    spread, w_query, w_key, w_value = together(to_pieces(layer_input[0]), w_query, w_key, w_value)
    x_own = to_plane(spread, jnp.arange(groups, dtype=jnp.int32))
    x_own, small_all = together(x_own, small_all)
    gain_rows, head_rows = attn_gain.shape[0], q_gain.shape[0]
    at = 0
    attn_gain_full = small_all[:, at : at + gain_rows].reshape(-1)
    at += gain_rows
    mlp_gain_full = small_all[:, at : at + gain_rows].reshape(-1)
    at += gain_rows
    q_gain_full = small_all[:, at : at + head_rows].reshape(-1)
    at += head_rows
    k_gain_full = small_all[:, at : at + head_rows].reshape(-1)
    at += head_rows
    whole = small_all[:, at:].astype(jnp.int32).reshape(groups, ring, 4)
    lengths_all = whole[:, 0, 0]
    order_all = whole[:, 0, 1]
    each = jnp.arange(groups, dtype=jnp.int32)
    slot_of = jnp.sum(jnp.where(order_all[None, :] == each[:, None], each[None, :], 0), axis=1)
    length = pick(lengths_all, plane)
    starts = pick(whole[:, :, 2:4], plane).reshape(groups, lanes, 2)
    starts = jnp.transpose(xor_order(starts, plane), (1, 2, 0))
    starts = jnp.transpose(xor_order(starts, lane), (1, 0, 2))
    starts = jnp.transpose(xor_order(starts, own // per_block), (1, 0, 2))
    flip = own % per_block
    tile_starts = starts[0].reshape(-1)
    block_starts = starts.reshape(-1)
    block_ids = jnp.arange(block_starts.shape[0], dtype=jnp.int32)
    block_at = jnp.sum(
        jnp.where(block_starts[None, :] == (block_ids * block_rows)[:, None], block_ids[None, :], 0), axis=1
    )
    meta = jnp.concatenate([length[None], flip[None].astype(jnp.int32), tile_starts, block_at])
    within = jnp.arange(block_rows, dtype=jnp.int32) ^ (flip * piece)
    positions = (
        starts[0][:, None, :, None] + within.reshape(1, per_block, 1, piece)
    ).reshape(groups, rows)
    valid_own = positions[0] < length

    def to_columns(parts):
        out = jnp.zeros((groups, shard_rows, sum(p.shape[1] for p in parts) // groups), BF)
        for k in steps:
            piece_k = jnp.concatenate(
                [
                    lax.dynamic_slice_in_dim(p, (own ^ k) * (p.shape[1] // groups), p.shape[1] // groups, 1)
                    for p in parts
                ],
                axis=1,
            )
            out = lax.dynamic_update_index_in_dim(out, swap(piece_k, k), own ^ k, 0)
        return out

    def from_columns(grad, widths):
        outs = [jnp.zeros((shard_rows, w * groups), F32) for w in widths]
        for k in steps:
            piece_k = swap(pick(grad, own ^ k), k).astype(F32)
            at = 0
            for n, w in enumerate(widths):
                outs[n] = lax.dynamic_update_slice_in_dim(outs[n], piece_k[:, at : at + w], (own ^ k) * w, 1)
                at += w
        return outs

    qkv_local = to_columns([w_query, w_key, w_value])
    qkv_local, x_own = together(qkv_local, x_own)
    w_qkv = lax.all_gather(qkv_local, "ctx", axis=1, tiled=True).reshape(width, -1)
    w_out_full = lax.all_gather(w_out, "ctx", axis=0, tiled=True)
    x_all = jnp.concatenate([swap(x_own, k) for k in steps], axis=0)
    cosine, sine = rope_tables(positions.reshape(-1))
    normed_one, proj, query_rot, kv_rot = project(
        x_all, attn_gain_full, w_qkv, cosine, sine, q_gain_full, k_gain_full, kv_width
    )
    w_gate, w_up, grad_out, normed_one = together(w_gate, w_up, grad_out, normed_one)
    gate_up_local = to_columns([w_gate, w_up])
    w_gate_up = lax.all_gather(gate_up_local, "ctx", axis=1, tiled=True).reshape(width, -1)
    w_down_full = lax.all_gather(w_down, "ctx", axis=0, tiled=True)
    tile_shape = (2, per_block, groups, piece, -1)
    queries = query_rot.reshape(tile_shape)
    kv_own = kv_rot.reshape(tile_shape)
    kv_all = jnp.stack([swap_lane(kv_own, k) for k in range(lanes)])
    mixture, logs = attention_forward(meta, queries, kv_all)
    mix_b = mixture.reshape(tokens, -1)
    attn_part = dot_nn(mix_b, w_out_full).reshape(groups, rows, width)
    hidden_res = x_own.astype(F32) + attn_part[0]
    for k in steps[1:]:
        hidden_res = hidden_res + swap(attn_part[k].astype(BF), k).astype(F32)
    normed_two_own = rms_scale(hidden_res, mlp_gain_full).astype(BF)
    normed_two = jnp.concatenate([swap(normed_two_own, k) for k in steps], axis=0)
    dy_own = to_plane(to_pieces(grad_out[0]), slot_of)
    dy_own = jnp.where(valid_own[:, None], dy_own, jnp.zeros((), BF))
    gate_up, dy_own = together(dot_nn(normed_two, w_gate_up), dy_own)
    gate_proj, up_proj = gate_up[:, :hidden], gate_up[:, hidden:]
    hidden_act = (jax.nn.silu(gate_proj) * up_proj).astype(BF)

    dy_b = jnp.concatenate([swap(dy_own, k) for k in steps], axis=0)
    grad_down_part, dy_after = together(dot_tn(hidden_act, dy_b).astype(BF), dy_b)
    grad_down = lax.psum_scatter(grad_down_part, "ctx", scatter_dimension=0, tiled=True)
    out_part = dot_nn(hidden_act, w_down_full).reshape(groups, rows, width)
    out_sent = [out_part[k].astype(BF) for k in steps[1:]]
    dy_after, *out_sent = together(dy_after, *out_sent)
    arrived = [swap(out_sent[k - 1], k) for k in steps[1:]]
    dhid = dot_nt(dy_after, w_down_full)
    _, swiglu_pull = jax.vjp(lambda g, u: jax.nn.silu(g) * u, gate_proj, up_proj)
    dgate_f, dup_f = swiglu_pull(dhid)
    dgate, dup, arrived[0] = together(dgate_f.astype(BF), dup_f.astype(BF), arrived[0])
    dn_two_part = dot_nt(jnp.concatenate([dgate, dup], axis=1), w_gate_up).reshape(groups, rows, width)
    dn_two_part, normed_two, *arrived = together(dn_two_part, normed_two, *arrived)
    result = out_part[0] + hidden_res
    for received in arrived:
        result = result + received.astype(F32)
    result = leave_plane(result.astype(BF).reshape(groups, piece, width))
    dn_two = dn_two_part[0]
    for k in steps[1:]:
        dn_two = dn_two + swap(dn_two_part[k].astype(BF), k).astype(F32)
    grad_gate = lax.psum_scatter(
        dot_tn(normed_two, dgate).astype(BF).reshape(groups, -1, hidden), "ctx", scatter_dimension=1, tiled=True
    )
    grad_up = lax.psum_scatter(
        dot_tn(normed_two, dup).astype(BF).reshape(groups, -1, hidden), "ctx", scatter_dimension=1, tiled=True
    )
    dn_two, grad_down = together(dn_two, grad_down)
    _, norm_two_pull = jax.vjp(rms_scale, hidden_res, mlp_gain_full)
    dh_norm, dmlp_gain_part = norm_two_pull(dn_two)
    dh_rows = dy_own.astype(F32) + dh_norm
    dattn_own = dh_rows.astype(BF)
    dattn_b = jnp.concatenate([swap(dattn_own, k) for k in steps], axis=0)
    dattn_b, grad_gate, result = together(dattn_b, grad_gate, result)
    result = from_plane(result, order_all)
    dmix_b = dot_nt(dattn_b, w_out_full).astype(BF)
    grad_out_w = lax.psum_scatter(dot_tn(mix_b, dattn_b).astype(BF), "ctx", scatter_dimension=0, tiled=True)

    dq_rot, dkv_parts = attention_backward(meta, queries, kv_all, dmix_b.reshape(queries.shape), mixture, logs)
    dkv_parts = dkv_parts.reshape(lanes, tokens, -1)
    other = swap_lane(dkv_parts[1], 1)
    for k in range(2, lanes):
        other = other + swap_lane(dkv_parts[k], k)
    dqkv, dhead_gains = unproject(
        dq_rot.reshape(tokens, -1), dkv_parts[0], other, proj, cosine, sine, q_gain_full, k_gain_full
    )

    dqkv, grad_up, result = together(dqkv, grad_up, result)
    dn_one_part = dot_nt(dqkv, w_qkv).reshape(groups, rows, width)
    dn_one_part, normed_one = together(dn_one_part, normed_one)
    grad_qkv_part = dot_tn(normed_one, dqkv).astype(BF).reshape(groups, -1, dqkv.shape[1])
    grad_qkv = lax.psum_scatter(grad_qkv_part, "ctx", scatter_dimension=1, tiled=True)
    dn_one = dn_one_part[0]
    for k in steps[1:]:
        dn_one = dn_one + swap(dn_one_part[k].astype(BF), k).astype(F32)
    dn_one, grad_out_w, grad_up = together(dn_one, grad_out_w, grad_up)
    _, norm_one_pull = jax.vjp(rms_scale, x_own.astype(F32), attn_gain_full)
    dflat_norm, dattn_gain_part = norm_one_pull(dn_one)
    grad_rows, dattn_gain_part = together((dh_rows + dflat_norm).astype(BF), dattn_gain_part)
    spread = leave_plane(grad_rows.reshape(groups, piece, width))
    grad_w_query, grad_w_key, grad_w_value = from_columns(grad_qkv, [q_width, kv_width, kv_width])
    spread, grad_w_query = together(spread, grad_w_query)
    grad_x = from_plane(spread, each)

    devices = groups * ring
    gains = jnp.concatenate(
        [
            dattn_gain_part.reshape(devices, -1),
            dmlp_gain_part.reshape(devices, -1),
            dhead_gains[0].reshape(devices, -1),
            dhead_gains[1].reshape(devices, -1),
        ],
        axis=1,
    )
    gains = scatter_all(gains)[0]
    grad_attn_gain = gains[:gain_rows]
    grad_mlp_gain = gains[gain_rows : 2 * gain_rows]
    grad_q_gain = gains[2 * gain_rows : 2 * gain_rows + head_rows]
    grad_k_gain = gains[2 * gain_rows + head_rows :]
    (grad_w_gate,) = from_columns(grad_gate, [hidden])
    (grad_w_up,) = from_columns(grad_up, [hidden])
    return (
        result,
        grad_x,
        grad_attn_gain,
        grad_w_query,
        grad_w_key,
        grad_w_value,
        grad_q_gain,
        grad_k_gain,
        grad_out_w.astype(F32),
        grad_mlp_gain,
        grad_w_gate,
        grad_w_up,
        grad_down.astype(F32),
    )


def solution(mesh):
    rows = P(("fsdp", "ctx"), None)
    vector = P(("fsdp", "ctx"))
    tokens = P("fsdp", "ctx", None)
    return jax.shard_map(
        per_device,
        mesh=mesh,
        in_specs=(
            tokens,
            P("fsdp"),
            P("fsdp"),
            P("fsdp", "ctx"),
            vector,
            rows,
            rows,
            rows,
            vector,
            vector,
            rows,
            vector,
            rows,
            rows,
            rows,
            tokens,
        ),
        out_specs=(
            tokens,
            tokens,
            vector,
            rows,
            rows,
            rows,
            vector,
            vector,
            rows,
            vector,
            rows,
            rows,
            rows,
        ),
        check_vma=False,
    )
```

```python
import functools

import jax
import jax.numpy as jnp
from jax import lax
from jax.experimental import pallas as pl
from jax.experimental.pallas import tpu as pltpu
from jax.sharding import PartitionSpec as P

H = 16
KVH = 8
HD = 128

EPS = 1e-06
THETA = 1000000.0
LOG2_E = 1.4426950408889634
STEP = 4
BF = jnp.bfloat16
F32 = jnp.float32


def rms_scale(values, gain):
    inverse = lax.rsqrt(jnp.mean(values * values, axis=-1, keepdims=True) + EPS)
    return values * inverse * gain


def rope_tables(positions):
    freqs = THETA ** (-(jnp.arange(HD // 2, dtype=F32) * 2.0) / HD)
    angles = positions.astype(F32)[:, None] * freqs
    cosine = jnp.cos(angles)
    sine = jnp.sin(angles)
    return (jnp.concatenate([cosine, cosine], axis=-1), jnp.concatenate([-sine, sine], axis=-1))


def dot_nn(left, right):
    return lax.dot_general(left, right, (((1,), (0,)), ((), ())), preferred_element_type=F32)


def dot_nt(left, right):
    return lax.dot_general(left, right, (((1,), (1,)), ((), ())), preferred_element_type=F32)


def dot_tn(left, right):
    return lax.dot_general(left, right, (((0,), (0,)), ((), ())), preferred_element_type=F32)


def pick(stacked, index):
    return lax.dynamic_index_in_dim(stacked, index, 0, keepdims=False)


def xor_order(stacked, index):
    count = stacked.shape[0]
    bit = 1
    while bit < count:
        paired = stacked.reshape((count // (2 * bit), 2, bit) + stacked.shape[1:])
        flipped = jnp.concatenate([paired[:, 1:], paired[:, :1]], axis=1).reshape(stacked.shape)
        stacked = jnp.where((index & bit) != 0, flipped, stacked)
        bit *= 2
    return stacked


def key_block(kv_ref, block, blocks, cols):
    kc, kfb, kz = block // (2 * blocks), (block // blocks) % 2, block % blocks
    taken = kv_ref[kc, kfb, :, kz, :, cols]
    return taken.reshape(taken.shape[0] * taken.shape[1], taken.shape[2])


def stack_heads(ref, kv_head, per_key):
    parts = []
    for head in range(kv_head * per_key, (kv_head + 1) * per_key):
        part = ref[0, :, 0, :, head * HD : (head + 1) * HD]
        parts.append(part.reshape(part.shape[0] * part.shape[1], HD))
    return jnp.concatenate(parts, axis=0)


def attn_fwd_kernel(meta, q_ref, kv_ref, o_ref, lse_ref, acc_ref, total_ref, *, kv_heads, per_key, blocks, piece):
    tile_rows = q_ref.shape[1] * piece
    stacked = per_key * tile_rows
    kv_width = kv_heads * HD
    tile = pl.program_id(0)
    length, flip, start = meta[0], meta[1] * piece, meta[2 + tile]
    ids = 2 + 2 * blocks
    row = lax.broadcasted_iota(jnp.int32, (stacked, 1), 0) % tile_rows
    row_limit = jnp.minimum(start + (row ^ flip), length - 1)
    column = lax.broadcasted_iota(jnp.int32, (1, STEP * tile_rows), 1) ^ flip
    last = jnp.minimum(start, length - 1) // tile_rows
    acc_ref[...] = jnp.zeros_like(acc_ref)
    total_ref[...] = jnp.zeros_like(total_ref)
    queries = [stack_heads(q_ref, h, per_key) for h in range(kv_heads)]

    def body(step, carry):
        taken = [meta[ids + STEP * step + n] for n in range(STEP)]
        allowed = step * (STEP * tile_rows) + column <= row_limit

        def columns_of(at):
            return jnp.concatenate([key_block(kv_ref, b, blocks, slice(at, at + HD)) for b in taken], axis=0)

        scores = [dot_nt(queries[h], columns_of(h * HD)) for h in range(kv_heads)]
        weights = [jnp.where(allowed, jnp.exp2(x * (HD ** (-0.5) * LOG2_E)), 0.0) for x in scores]
        parts = [dot_nn(weights[h].astype(BF), columns_of(kv_width + h * HD)) for h in range(kv_heads)]
        for h in range(kv_heads):
            part = weights[h][:, :HD]
            for at in range(HD, STEP * tile_rows, HD):
                part = part + weights[h][:, at : at + HD]
            total_ref[h] += part
            acc_ref[h] += parts[h]
        return carry

    lax.fori_loop(0, last // STEP + 1, body, 0)
    for h in range(kv_heads):
        total = jnp.sum(total_ref[h], axis=1, keepdims=True)
        out = (acc_ref[h] / total).astype(BF)
        for g in range(per_key):
            head = h * per_key + g
            o_ref[0, :, 0, :, head * HD : (head + 1) * HD] = out[g * tile_rows : (g + 1) * tile_rows].reshape(
                -1, piece, HD
            )
        lse_ref[0, h] = jnp.log2(jnp.sum(total_ref[h].T, axis=0, keepdims=True))


def attn_bwd_kernel(
    meta, q_ref, kv_ref, do_ref, o_ref, lse_ref, dq_ref, dkv_ref, sum_ref, dq_sum_ref, *, kv_heads, per_key, blocks, piece
):
    tile_rows = q_ref.shape[1] * piece
    stacked = per_key * tile_rows
    kv_width = kv_heads * HD
    tile = pl.program_id(0)
    length, flip, start = meta[0], meta[1] * piece, meta[2 + tile]
    ids = 2 + 2 * blocks
    row = lax.broadcasted_iota(jnp.int32, (1, stacked), 1) % tile_rows
    row_limit = jnp.minimum(start + (row ^ flip), length - 1)
    column = lax.broadcasted_iota(jnp.int32, (STEP * tile_rows, 1), 0) ^ flip
    score_scale = HD ** (-0.5)

    @pl.when(tile == 0)
    def _():
        sum_ref[...] = jnp.zeros_like(sum_ref)

    dq_sum_ref[...] = jnp.zeros_like(dq_sum_ref)
    queries = [stack_heads(q_ref, h, per_key) for h in range(kv_heads)]
    grads = [stack_heads(do_ref, h, per_key) for h in range(kv_heads)]
    deltas = [
        jnp.sum((grads[h].astype(F32) * stack_heads(o_ref, h, per_key).astype(F32)).T, axis=0, keepdims=True)
        for h in range(kv_heads)
    ]
    logs = [lse_ref[0, h] for h in range(kv_heads)]

    def body(step, carry):
        taken = [meta[ids + STEP * step + n] for n in range(STEP)]
        allowed = step * (STEP * tile_rows) + column <= row_limit

        def columns_of(at):
            return jnp.concatenate([key_block(kv_ref, b, blocks, slice(at, at + HD)) for b in taken], axis=0)

        each = range(kv_heads)
        keys = [columns_of(h * HD) for h in each]
        scores = [dot_nt(keys[h], queries[h]) for h in each]
        dprobs = [dot_nt(columns_of(kv_width + h * HD), grads[h]) for h in each]
        probs = [
            jnp.where(allowed, jnp.exp2(scores[h] * (score_scale * LOG2_E) - logs[h]), 0.0) for h in each
        ]
        dscores = [(probs[h] * (dprobs[h] - deltas[h])).astype(BF) for h in each]
        dvs = [dot_nn(probs[h].astype(BF), grads[h]) for h in each]
        dks = [dot_nn(dscores[h], queries[h]) for h in each]
        dqs = [dot_tn(dscores[h], keys[h]) for h in each]
        for h in each:
            dq_sum_ref[h] += dqs[h]
            for n, block in enumerate(taken):
                part = slice(n * tile_rows, (n + 1) * tile_rows)
                sum_ref[block, :, h * HD : (h + 1) * HD] += dks[h][part]
                sum_ref[block, :, kv_width + h * HD : kv_width + (h + 1) * HD] += dvs[h][part]
        return carry

    lax.fori_loop(0, jnp.where(start < length, start // tile_rows // STEP + 1, 0), body, 0)
    for h in range(kv_heads):
        for g in range(per_key):
            head = h * per_key + g
            dq_ref[0, :, 0, :, head * HD : (head + 1) * HD] = (
                dq_sum_ref[h, g * tile_rows : (g + 1) * tile_rows] * score_scale
            ).reshape(-1, piece, HD)

    @pl.when(tile == pl.num_programs(0) - 1)
    def _():
        for kc in range(dkv_ref.shape[0]):
            for kfb in range(2):
                for kz in range(blocks):
                    block = (kc * 2 + kfb) * blocks + kz
                    dkv_ref[kc, kfb, :, kz, :, :kv_width] = (
                        (sum_ref[block, :, :kv_width] * score_scale).astype(BF).reshape(-1, piece, kv_width)
                    )
                    dkv_ref[kc, kfb, :, kz, :, kv_width:] = (
                        sum_ref[block, :, kv_width:].astype(BF).reshape(-1, piece, kv_width)
                    )


def attention_specs(queries, kv_all):
    halves, per_block, blocks, piece, q_width = queries.shape
    tile_spec = pl.BlockSpec((1, per_block, 1, piece, q_width), lambda t, meta: (t // blocks, 0, t % blocks, 0, 0))
    kv_spec = pl.BlockSpec(kv_all.shape, lambda t, meta: (0,) * 6)
    kv_heads = kv_all.shape[-1] // (2 * HD)
    per_key = q_width // HD // kv_heads
    lse_spec = pl.BlockSpec((1, kv_heads, 1, per_key * per_block * piece), lambda t, meta: (t, 0, 0, 0))
    sizes = dict(kv_heads=kv_heads, per_key=per_key, blocks=blocks, piece=piece)
    return halves * blocks, tile_spec, kv_spec, lse_spec, sizes, per_block * piece


def attention_forward(meta, queries, kv_all):
    tiles, tile_spec, kv_spec, lse_spec, sizes, tile_rows = attention_specs(queries, kv_all)
    kv_heads, per_key = sizes["kv_heads"], sizes["per_key"]
    stacked = per_key * tile_rows
    pairs = tiles * kv_heads * stacked * tiles * 2 * tile_rows // 2
    return pl.pallas_call(
        functools.partial(attn_fwd_kernel, **sizes),
        grid_spec=pltpu.PrefetchScalarGridSpec(
            num_scalar_prefetch=1,
            grid=(tiles,),
            in_specs=[tile_spec, kv_spec],
            out_specs=[tile_spec, lse_spec],
            scratch_shapes=[
                pltpu.VMEM((kv_heads, stacked, HD), F32),
                pltpu.VMEM((kv_heads, stacked, HD), F32),
            ],
        ),
        out_shape=[
            jax.ShapeDtypeStruct(queries.shape, BF),
            jax.ShapeDtypeStruct((tiles, kv_heads, 1, stacked), F32),
        ],
        cost_estimate=pl.CostEstimate(flops=pairs * HD * 4, transcendentals=pairs, bytes_accessed=4 * kv_all.size),
    )(meta, queries, kv_all)


def attention_backward(meta, queries, kv_all, dmix, mixture, logs):
    tiles, tile_spec, kv_spec, lse_spec, sizes, tile_rows = attention_specs(queries, kv_all)
    kv_heads, per_key = sizes["kv_heads"], sizes["per_key"]
    stacked = per_key * tile_rows
    key_blocks = kv_all.shape[0] * tiles
    pairs = tiles * kv_heads * stacked * tiles * 2 * tile_rows // 2
    return pl.pallas_call(
        functools.partial(attn_bwd_kernel, **sizes),
        grid_spec=pltpu.PrefetchScalarGridSpec(
            num_scalar_prefetch=1,
            grid=(tiles,),
            in_specs=[tile_spec, kv_spec, tile_spec, tile_spec, lse_spec],
            out_specs=[tile_spec, kv_spec],
            scratch_shapes=[
                pltpu.VMEM((key_blocks, tile_rows, kv_all.shape[-1]), F32),
                pltpu.VMEM((kv_heads, stacked, HD), F32),
            ],
        ),
        out_shape=[
            jax.ShapeDtypeStruct(queries.shape, F32),
            jax.ShapeDtypeStruct(kv_all.shape, BF),
        ],
        cost_estimate=pl.CostEstimate(flops=pairs * HD * 10, transcendentals=pairs, bytes_accessed=10 * kv_all.size),
    )(meta, queries, kv_all, dmix, mixture, logs)


def turned(values):
    return pltpu.roll(values, HD // 2, axis=1)


def project_kernel(
    x_ref, gain_ref, w_ref, cos_ref, sin_ref, q_gain_ref, k_gain_ref, normed_ref, proj_ref, q_ref, kv_ref, *, kv_width
):
    q_width = q_ref.shape[1]
    normed_ref[...] = rms_scale(x_ref[...].astype(F32), gain_ref[...]).astype(BF)
    proj = dot_nn(normed_ref[...], w_ref[...])
    proj_ref[...] = proj[:, : q_width + kv_width]
    cosine, sine = cos_ref[...], sin_ref[...]
    for at in range(0, q_width + kv_width, HD):
        gain = q_gain_ref[...] if at < q_width else k_gain_ref[...]
        normed = rms_scale(proj[:, at : at + HD], gain)
        rotated = (normed * cosine + turned(normed) * sine).astype(BF)
        if at < q_width:
            q_ref[:, at : at + HD] = rotated
        else:
            kv_ref[:, at - q_width : at - q_width + HD] = rotated
    kv_ref[:, kv_width:] = proj[:, q_width + kv_width :].astype(BF)


def project(x_all, attn_gain, w_qkv, cosine, sine, q_gain, k_gain, kv_width):
    tokens, width = x_all.shape
    columns = w_qkv.shape[1]
    q_width = columns - 2 * kv_width
    tile = min(256, tokens)

    def rows(n):
        return pl.BlockSpec((tile, n), lambda i: (i, 0))

    def whole(*shape):
        return pl.BlockSpec(shape, lambda i: (0, 0))

    return pl.pallas_call(
        functools.partial(project_kernel, kv_width=kv_width),
        grid=(tokens // tile,),
        in_specs=[rows(width), whole(1, width), whole(width, columns), rows(HD), rows(HD), whole(1, HD), whole(1, HD)],
        out_specs=[rows(width), rows(q_width + kv_width), rows(q_width), rows(2 * kv_width)],
        out_shape=[
            jax.ShapeDtypeStruct((tokens, width), BF),
            jax.ShapeDtypeStruct((tokens, q_width + kv_width), F32),
            jax.ShapeDtypeStruct((tokens, q_width), BF),
            jax.ShapeDtypeStruct((tokens, 2 * kv_width), BF),
        ],
        cost_estimate=pl.CostEstimate(
            flops=2 * tokens * width * columns, transcendentals=0, bytes_accessed=8 * tokens * width
        ),
    )(x_all, attn_gain[None], w_qkv, cosine, sine, q_gain[None], k_gain[None])


def unproject_kernel(
    dq_ref, dkv_ref, other_ref, proj_ref, cos_ref, sin_ref, q_gain_ref, k_gain_ref, dqkv_ref, dgain_ref, *, kv_width
):
    q_width = dq_ref.shape[1]

    @pl.when(pl.program_id(0) == 0)
    def _():
        dgain_ref[...] = jnp.zeros_like(dgain_ref)

    cosine, sine = cos_ref[...], sin_ref[...]
    dkv = dkv_ref[...].astype(F32) + other_ref[...].astype(F32)
    for at in range(0, q_width + kv_width, HD):
        is_q = at < q_width
        grad = dq_ref[:, at : at + HD] if is_q else dkv[:, at - q_width : at - q_width + HD]
        gain = q_gain_ref[...] if is_q else k_gain_ref[...]
        values = proj_ref[:, at : at + HD]
        inverse = lax.rsqrt(jnp.mean(values * values, axis=1, keepdims=True) + EPS)
        dnormed = grad * cosine + turned(grad * sine)
        n = 0 if is_q else 1
        dgain_ref[n : n + 1] += jnp.sum(dnormed * values * inverse, axis=0, keepdims=True)
        scaled = dnormed * gain
        inner = jnp.mean(scaled * values, axis=1, keepdims=True)
        dqkv_ref[:, at : at + HD] = (inverse * scaled - values * (inverse * inverse * inverse * inner)).astype(BF)
    dqkv_ref[:, q_width + kv_width :] = dkv[:, kv_width:].astype(BF)


def unproject(dq, dkv, other, proj, cosine, sine, q_gain, k_gain):
    tokens, q_width = dq.shape
    kv_width = dkv.shape[1] // 2
    columns = q_width + 2 * kv_width
    tile = min(256, tokens)

    def rows(n):
        return pl.BlockSpec((tile, n), lambda i: (i, 0))

    def whole(*shape):
        return pl.BlockSpec(shape, lambda i: (0, 0))

    return pl.pallas_call(
        functools.partial(unproject_kernel, kv_width=kv_width),
        grid=(tokens // tile,),
        in_specs=[
            rows(q_width),
            rows(2 * kv_width),
            rows(2 * kv_width),
            rows(q_width + kv_width),
            rows(HD),
            rows(HD),
            whole(1, HD),
            whole(1, HD),
        ],
        out_specs=[rows(columns), whole(2, HD)],
        out_shape=[jax.ShapeDtypeStruct((tokens, columns), BF), jax.ShapeDtypeStruct((2, HD), F32)],
        cost_estimate=pl.CostEstimate(
            flops=30 * tokens * columns, transcendentals=0, bytes_accessed=12 * tokens * columns
        ),
    )(dq, dkv, other, proj, cosine, sine, q_gain[None], k_gain[None])


def together(*values):
    return lax.optimization_barrier(values)


def per_device(
    layer_input,
    lengths,
    order,
    offsets,
    attn_gain,
    w_query,
    w_key,
    w_value,
    q_gain,
    k_gain,
    w_out,
    mlp_gain,
    w_gate,
    w_up,
    w_down,
    grad_out,
):
    groups, ring = lax.axis_size("fsdp"), lax.axis_size("ctx")
    _, rows, width = layer_input.shape
    lanes = ring // groups
    piece, block_rows = rows // groups, rows // 2
    per_block = block_rows // piece
    heads, kv_heads = H // groups, KVH // groups
    q_width, kv_width = heads * HD, kv_heads * HD
    shard_rows = w_query.shape[0]
    hidden = w_gate.shape[1] // groups
    own = lax.axis_index("fsdp")
    own_ctx = lax.axis_index("ctx")
    plane, lane = own_ctx // lanes, own_ctx % lanes
    steps = range(groups)
    tokens = groups * rows

    def swap(block, step):
        if step == 0:
            return block
        return lax.ppermute(block, "fsdp", [(i, i ^ step) for i in range(groups)])

    def swap_plane(block, step):
        if step == 0:
            return block
        return lax.ppermute(block, "ctx", [(i, (i // lanes ^ step) * lanes + i % lanes) for i in range(ring)])

    def swap_lane(block, step):
        if step == 0:
            return block
        return lax.ppermute(block, "ctx", [(i, i // lanes * lanes + (i % lanes ^ step)) for i in range(ring)])

    def gather_all(part):
        for axis, index, count in (("ctx", own_ctx, ring), ("fsdp", own, groups)):
            step = 1
            while step < count:
                other = lax.ppermute(part, axis, [(i, i ^ step) for i in range(count)])
                low = (index & step) == 0
                part = jnp.concatenate([jnp.where(low, part, other), jnp.where(low, other, part)], axis=0)
                step *= 2
        return part

    def scatter_all(part):
        for axis, index, count in (("fsdp", own, groups), ("ctx", own_ctx, ring)):
            step = count // 2
            while step:
                half = part.shape[0] // 2
                low = (index & step) == 0
                kept = jnp.where(low, part[:half], part[half:])
                sent = jnp.where(low, part[half:], part[:half])
                part = kept + lax.ppermute(sent, axis, [(i, i ^ step) for i in range(count)])
                step //= 2
        return part

    def to_pieces(local):
        pieces = local.reshape(groups, piece, width)
        return jnp.stack([swap(pick(pieces, own ^ k), k) for k in steps])

    def to_plane(spread, holder):
        mine = [swap_plane(pick(spread, own ^ holder[plane ^ k]), k) for k in steps]
        return jnp.concatenate(mine, axis=0)

    def leave_plane(mine):
        return jnp.stack([swap_plane(mine[k], k) for k in steps])

    def from_plane(spread, held):
        back = jnp.stack([swap(pick(spread, plane ^ held[own ^ k]), k) for k in steps])
        return xor_order(back, own).reshape(1, rows, width)

    small = jnp.concatenate(
        [
            attn_gain.astype(F32),
            mlp_gain.astype(F32),
            q_gain.astype(F32),
            k_gain.astype(F32),
            lengths.astype(F32),
            order.astype(F32),
            offsets.reshape(-1).astype(F32),
        ]
    )[None, :]
    small_all = gather_all(small)
    spread, w_query, w_key, w_value = together(to_pieces(layer_input[0]), w_query, w_key, w_value)
    x_own = to_plane(spread, jnp.arange(groups, dtype=jnp.int32))
    x_own, small_all = together(x_own, small_all)
    gain_rows, head_rows = attn_gain.shape[0], q_gain.shape[0]
    at = 0
    attn_gain_full = small_all[:, at : at + gain_rows].reshape(-1)
    at += gain_rows
    mlp_gain_full = small_all[:, at : at + gain_rows].reshape(-1)
    at += gain_rows
    q_gain_full = small_all[:, at : at + head_rows].reshape(-1)
    at += head_rows
    k_gain_full = small_all[:, at : at + head_rows].reshape(-1)
    at += head_rows
    whole = small_all[:, at:].astype(jnp.int32).reshape(groups, ring, 4)
    lengths_all = whole[:, 0, 0]
    order_all = whole[:, 0, 1]
    each = jnp.arange(groups, dtype=jnp.int32)
    slot_of = jnp.sum(jnp.where(order_all[None, :] == each[:, None], each[None, :], 0), axis=1)
    length = pick(lengths_all, plane)
    starts = pick(whole[:, :, 2:4], plane).reshape(groups, lanes, 2)
    starts = jnp.transpose(xor_order(starts, plane), (1, 2, 0))
    starts = jnp.transpose(xor_order(starts, lane), (1, 0, 2))
    starts = jnp.transpose(xor_order(starts, own // per_block), (1, 0, 2))
    flip = own % per_block
    tile_starts = starts[0].reshape(-1)
    block_starts = starts.reshape(-1)
    block_ids = jnp.arange(block_starts.shape[0], dtype=jnp.int32)
    block_at = jnp.sum(
        jnp.where(block_starts[None, :] == (block_ids * block_rows)[:, None], block_ids[None, :], 0), axis=1
    )
    meta = jnp.concatenate([length[None], flip[None].astype(jnp.int32), tile_starts, block_at])
    within = jnp.arange(block_rows, dtype=jnp.int32) ^ (flip * piece)
    positions = (
        starts[0][:, None, :, None] + within.reshape(1, per_block, 1, piece)
    ).reshape(groups, rows)
    valid_own = positions[0] < length

    def to_columns(parts):
        out = jnp.zeros((groups, shard_rows, sum(p.shape[1] for p in parts) // groups), BF)
        for k in steps:
            piece_k = jnp.concatenate(
                [
                    lax.dynamic_slice_in_dim(p, (own ^ k) * (p.shape[1] // groups), p.shape[1] // groups, 1)
                    for p in parts
                ],
                axis=1,
            )
            out = lax.dynamic_update_index_in_dim(out, swap(piece_k, k), own ^ k, 0)
        return out

    def from_columns(grad, widths):
        outs = [jnp.zeros((shard_rows, w * groups), F32) for w in widths]
        for k in steps:
            piece_k = swap(pick(grad, own ^ k), k).astype(F32)
            at = 0
            for n, w in enumerate(widths):
                outs[n] = lax.dynamic_update_slice_in_dim(outs[n], piece_k[:, at : at + w], (own ^ k) * w, 1)
                at += w
        return outs

    qkv_local = to_columns([w_query, w_key, w_value])
    qkv_local, x_own = together(qkv_local, x_own)
    w_qkv = lax.all_gather(qkv_local, "ctx", axis=1, tiled=True).reshape(width, -1)
    w_out_full = lax.all_gather(w_out, "ctx", axis=0, tiled=True)
    x_all = jnp.concatenate([swap(x_own, k) for k in steps], axis=0)
    cosine, sine = rope_tables(positions.reshape(-1))
    normed_one, proj, query_rot, kv_rot = project(
        x_all, attn_gain_full, w_qkv, cosine, sine, q_gain_full, k_gain_full, kv_width
    )
    w_gate, w_up, grad_out, normed_one = together(w_gate, w_up, grad_out, normed_one)
    gate_up_local = to_columns([w_gate, w_up])
    w_gate_up = lax.all_gather(gate_up_local, "ctx", axis=1, tiled=True).reshape(width, -1)
    w_down_full = lax.all_gather(w_down, "ctx", axis=0, tiled=True)
    tile_shape = (2, per_block, groups, piece, -1)
    queries = query_rot.reshape(tile_shape)
    kv_own = kv_rot.reshape(tile_shape)
    kv_all = jnp.stack([swap_lane(kv_own, k) for k in range(lanes)])
    mixture, logs = attention_forward(meta, queries, kv_all)
    mix_b = mixture.reshape(tokens, -1)
    attn_part = dot_nn(mix_b, w_out_full).reshape(groups, rows, width)
    hidden_res = x_own.astype(F32) + attn_part[0]
    for k in steps[1:]:
        hidden_res = hidden_res + swap(attn_part[k].astype(BF), k).astype(F32)
    normed_two_own = rms_scale(hidden_res, mlp_gain_full).astype(BF)
    normed_two = jnp.concatenate([swap(normed_two_own, k) for k in steps], axis=0)
    dy_own = to_plane(to_pieces(grad_out[0]), slot_of)
    dy_own = jnp.where(valid_own[:, None], dy_own, jnp.zeros((), BF))
    gate_up, dy_own = together(dot_nn(normed_two, w_gate_up), dy_own)
    gate_proj, up_proj = gate_up[:, :hidden], gate_up[:, hidden:]
    hidden_act = (jax.nn.silu(gate_proj) * up_proj).astype(BF)

    dy_b = jnp.concatenate([swap(dy_own, k) for k in steps], axis=0)
    grad_down_part, dy_after = together(dot_tn(hidden_act, dy_b).astype(BF), dy_b)
    grad_down = lax.psum_scatter(grad_down_part, "ctx", scatter_dimension=0, tiled=True)
    out_part = dot_nn(hidden_act, w_down_full).reshape(groups, rows, width)
    out_sent = [out_part[k].astype(BF) for k in steps[1:]]
    dy_after, *out_sent = together(dy_after, *out_sent)
    arrived = [swap(out_sent[k - 1], k) for k in steps[1:]]
    dhid = dot_nt(dy_after, w_down_full)
    _, swiglu_pull = jax.vjp(lambda g, u: jax.nn.silu(g) * u, gate_proj, up_proj)
    dgate_f, dup_f = swiglu_pull(dhid)
    dgate, dup, arrived[0] = together(dgate_f.astype(BF), dup_f.astype(BF), arrived[0])
    dn_two_part = dot_nt(jnp.concatenate([dgate, dup], axis=1), w_gate_up).reshape(groups, rows, width)
    dn_two_part, normed_two, *arrived = together(dn_two_part, normed_two, *arrived)
    result = out_part[0] + hidden_res
    for received in arrived:
        result = result + received.astype(F32)
    result = leave_plane(result.astype(BF).reshape(groups, piece, width))
    dn_two = dn_two_part[0]
    for k in steps[1:]:
        dn_two = dn_two + swap(dn_two_part[k].astype(BF), k).astype(F32)
    grad_gate = lax.psum_scatter(
        dot_tn(normed_two, dgate).astype(BF).reshape(groups, -1, hidden), "ctx", scatter_dimension=1, tiled=True
    )
    grad_up = lax.psum_scatter(
        dot_tn(normed_two, dup).astype(BF).reshape(groups, -1, hidden), "ctx", scatter_dimension=1, tiled=True
    )
    dn_two, grad_down = together(dn_two, grad_down)
    _, norm_two_pull = jax.vjp(rms_scale, hidden_res, mlp_gain_full)
    dh_norm, dmlp_gain_part = norm_two_pull(dn_two)
    dh_rows = dy_own.astype(F32) + dh_norm
    dattn_own = dh_rows.astype(BF)
    dattn_b = jnp.concatenate([swap(dattn_own, k) for k in steps], axis=0)
    dattn_b, grad_gate, result = together(dattn_b, grad_gate, result)
    result = from_plane(result, order_all)
    dmix_b = dot_nt(dattn_b, w_out_full).astype(BF)
    grad_out_w = lax.psum_scatter(dot_tn(mix_b, dattn_b).astype(BF), "ctx", scatter_dimension=0, tiled=True)

    dq_rot, dkv_parts = attention_backward(meta, queries, kv_all, dmix_b.reshape(queries.shape), mixture, logs)
    dkv_parts = dkv_parts.reshape(lanes, tokens, -1)
    other = swap_lane(dkv_parts[1], 1)
    for k in range(2, lanes):
        other = other + swap_lane(dkv_parts[k], k)
    dqkv, dhead_gains = unproject(
        dq_rot.reshape(tokens, -1), dkv_parts[0], other, proj, cosine, sine, q_gain_full, k_gain_full
    )

    dqkv, grad_up, result = together(dqkv, grad_up, result)
    dn_one_part = dot_nt(dqkv, w_qkv).reshape(groups, rows, width)
    dn_one_part, normed_one = together(dn_one_part, normed_one)
    grad_qkv_part = dot_tn(normed_one, dqkv).astype(BF).reshape(groups, -1, dqkv.shape[1])
    grad_qkv = lax.psum_scatter(grad_qkv_part, "ctx", scatter_dimension=1, tiled=True)
    dn_one = dn_one_part[0]
    for k in steps[1:]:
        dn_one = dn_one + swap(dn_one_part[k].astype(BF), k).astype(F32)
    dn_one, grad_out_w, grad_up = together(dn_one, grad_out_w, grad_up)
    _, norm_one_pull = jax.vjp(rms_scale, x_own.astype(F32), attn_gain_full)
    dflat_norm, dattn_gain_part = norm_one_pull(dn_one)
    spread = leave_plane((dh_rows + dflat_norm).astype(BF).reshape(groups, piece, width))
    grad_w_query, grad_w_key, grad_w_value = from_columns(grad_qkv, [q_width, kv_width, kv_width])
    spread, grad_w_query, dattn_gain_part = together(spread, grad_w_query, dattn_gain_part)
    grad_x = from_plane(spread, each)

    devices = groups * ring
    gains = jnp.concatenate(
        [
            dattn_gain_part.reshape(devices, -1),
            dmlp_gain_part.reshape(devices, -1),
            dhead_gains[0].reshape(devices, -1),
            dhead_gains[1].reshape(devices, -1),
        ],
        axis=1,
    )
    gains = scatter_all(gains)[0]
    grad_attn_gain = gains[:gain_rows]
    grad_mlp_gain = gains[gain_rows : 2 * gain_rows]
    grad_q_gain = gains[2 * gain_rows : 2 * gain_rows + head_rows]
    grad_k_gain = gains[2 * gain_rows + head_rows :]
    (grad_w_gate,) = from_columns(grad_gate, [hidden])
    (grad_w_up,) = from_columns(grad_up, [hidden])
    return (
        result,
        grad_x,
        grad_attn_gain,
        grad_w_query,
        grad_w_key,
        grad_w_value,
        grad_q_gain,
        grad_k_gain,
        grad_out_w.astype(F32),
        grad_mlp_gain,
        grad_w_gate,
        grad_w_up,
        grad_down.astype(F32),
    )


def solution(mesh):
    rows = P(("fsdp", "ctx"), None)
    vector = P(("fsdp", "ctx"))
    tokens = P("fsdp", "ctx", None)
    return jax.shard_map(
        per_device,
        mesh=mesh,
        in_specs=(
            tokens,
            P("fsdp"),
            P("fsdp"),
            P("fsdp", "ctx"),
            vector,
            rows,
            rows,
            rows,
            vector,
            vector,
            rows,
            vector,
            rows,
            rows,
            rows,
            tokens,
        ),
        out_specs=(
            tokens,
            tokens,
            vector,
            rows,
            rows,
            rows,
            vector,
            vector,
            rows,
            vector,
            rows,
            rows,
            rows,
        ),
        check_vma=False,
    )
```
